256 devices in a mesh: branch: 2 (over core), prow: 16 (over x, z_lo), pcol: 8 (over z_hi, y).
Axes of the slice: x: 4, y: 4, z: 8 (z_hi: 2, z_lo: 4; z = z_hi * 4 + z_lo), core: 2. Of those that a mesh axis runs over, the one named last changes fastest.
Arguments:
- pair_rep: float32 [256, 256, 128], P(('branch', 'prow'), 'pcol'), may hold values from -6 to 6
- alignment: float32 [32, 256, 256], P('pcol', ('branch', 'prow')), may hold values from -6 to 6
- residue_mask: int32 [256], replicated, may hold values 0 or 1
- row_mask: int32 [32, 256], P('pcol', ('branch', 'prow')), may hold values 0 or 1
- attention_in: float32 [256, 1024], replicated, may hold values from -0.375 to 0.375
- pair_bias_w: float32 [128, 8], replicated, may hold values from -40 to 40
- attention_out: float32 [256, 256], replicated, may hold values from -0.375 to 0.375
- outer_in: float32 [256, 64], replicated, may hold values from -0.375 to 0.375
- outer_out: float32 [1024, 128], replicated, may hold values from -0.1875 to 0.1875
- triangle_in: float32 [128, 512], replicated, may hold values from -0.5 to 0.5
- triangle_gate: float32 [128, 128], replicated, may hold values from -0.5 to 0.5
- triangle_out: float32 [128, 128], replicated, may hold values from -0.5 to 0.5
- transit_in: float32 [128, 512], replicated, may hold values from -0.5 to 0.5
- transit_out: float32 [512, 128], replicated, may hold values from -0.25 to 0.25
Outputs:
- new_alignment: float32 [32, 256, 256], P('pcol', ('branch', 'prow'))
- new_pair: float32 [256, 256, 128], P(('branch', 'prow'), 'pcol')
The draws below stay inside these ranges and needn't reach their ends.
All inputs are finite; a program needn't handle non-finite values. No bound on the sum of `row_mask` on one device may be relied on, other than what follows from the above.
Results may differ from the reference program's by a relative error of at most 0.0003.
Values sent between devices are 32-bit elements; how exact they have to be, the bound alone decides.
No kernel may reach another device: no remote copies, remote signals or barrier semaphores. Data moves between devices by JAX's collectives and lax.ppermute only.
A program may use at most 64 MiB of HBM per device.

```python
import jax
import jax.numpy as jnp
from jax import lax

CZ = 128
CM = 256
HEADS = 8
TRI = 128
TRANS = 512
OUTER = 32
ATT = 256
R = 256
S = 32


def draw_pair_bias_w(key, part):
    sample = jax.random.normal(key, (CZ, HEADS), jnp.float32)
    sample = sample * (2.0 / CZ ** 0.5)
    return jnp.clip(sample, -40.0, 40.0)


def place_ends(entries, stream_key, low, top_value):
    spot = [jax.random.randint(jax.random.fold_in(stream_key, axis), (), 0, length) for axis, length in enumerate(entries.shape)]
    longest = entries.shape.index(max(entries.shape))
    beside = spot[:longest] + [(spot[longest] + 1) % entries.shape[longest]] + spot[longest + 1:]
    return entries.at[tuple(spot)].set(low).at[tuple(beside)].set(top_value)


def block_scale(key, dims, split, low, largest):
    level, own = 1.0, jax.random.fold_in(key, 6)
    for dim, shards_of in split:
        heights = jnp.exp(jax.random.uniform(jax.random.fold_in(own, dim), (shards_of,), jnp.float32, low / len(split), largest / len(split)))
        level = level * jnp.repeat(heights, dims[dim] // shards_of).reshape([-1 if axis == dim else 1 for axis in range(len(dims))])
    return level


def noise(key, extent, deviation, reach, shards=(), held_as=jnp.bfloat16):
    factor_of = block_scale(key, extent, shards, -0.22, 0.18) if shards else 1.0
    result = jax.random.normal(key, extent, jnp.float32) * deviation * factor_of
    return jnp.minimum(jnp.maximum(result, -reach), reach).astype(held_as)


def setup_inputs(seed: int = 0) -> dict:
    keys = jax.random.split(jax.random.key(seed), 15)
    pair_rep = noise(keys[0], (R, R, CZ), 1.0, 6.0, ((0, 32), (1, 8)), jnp.float32)
    alignment = noise(keys[1], (S, R, CM), 1.0, 6.0, ((0, 8), (1, 32)), jnp.float32)
    residue_mask = place_ends((jax.random.randint(keys[2], (R,), 0, 8) < 7).astype(jnp.int32), jax.random.fold_in(keys[2], 1), 0, 1)
    row_mask = place_ends((jax.random.randint(keys[3], (S, R), 0, 4) < 3).astype(jnp.int32), jax.random.fold_in(keys[3], 1), 0, 1)
    attention_in = noise(keys[4], (CM, 4 * ATT), CM ** -0.5, 0.375, (), jnp.float32)
    pair_bias_w = draw_pair_bias_w(jax.random.fold_in(keys[14], 71), 0)
    attention_out = noise(keys[6], (ATT, CM), ATT ** -0.5, 0.375, (), jnp.float32)
    outer_in = noise(keys[7], (CM, 2 * OUTER), CM ** -0.5, 0.375, (), jnp.float32)
    outer_out = noise(keys[8], (OUTER * OUTER, CZ), (OUTER * OUTER) ** -0.5, 0.1875, (), jnp.float32)
    triangle_in = noise(keys[9], (CZ, 4 * TRI), CZ ** -0.5, 0.5, (), jnp.float32)
    triangle_gate = noise(keys[10], (CZ, CZ), CZ ** -0.5, 0.5, (), jnp.float32)
    triangle_out = noise(keys[11], (TRI, CZ), TRI ** -0.5, 0.5, (), jnp.float32)
    transit_in = noise(keys[12], (CZ, TRANS), CZ ** -0.5, 0.5, (), jnp.float32)
    transit_out = noise(keys[13], (TRANS, CZ), TRANS ** -0.5, 0.25, (), jnp.float32)
    return dict(pair_rep=pair_rep, alignment=alignment, residue_mask=residue_mask, row_mask=row_mask, attention_in=attention_in, pair_bias_w=pair_bias_w, attention_out=attention_out, outer_in=outer_in, outer_out=outer_out, triangle_in=triangle_in, triangle_gate=triangle_gate, triangle_out=triangle_out, transit_in=transit_in, transit_out=transit_out)


highest = lax.Precision.HIGHEST
epsilon = 1e-05

def layer_norm(values):
    center = values - lax.optimization_barrier(jnp.mean(values, axis=-1, keepdims=True))
    spread = lax.optimization_barrier(jnp.mean(center * center, axis=-1, keepdims=True))
    return center * lax.rsqrt(spread + epsilon)

def matmul(left_side, right_side):
    return jnp.dot(left_side, right_side, precision=highest, preferred_element_type=jnp.float32)

def reference(pair_rep, alignment, residue_mask, row_mask, attention_in, pair_bias_w, attention_out, outer_in, outer_out, triangle_in, triangle_gate, triangle_out, transit_in, transit_out):
    res_count = alignment.shape[1]
    head_count = pair_bias_w.shape[1]
    att_width = attention_out.shape[0]
    head_depth = att_width // head_count
    outer_width = outer_in.shape[1] // 2
    inner_width = triangle_out.shape[0]
    normed = layer_norm(alignment)
    projected = matmul(normed, attention_in)
    queries = projected[..., :att_width] * head_depth ** (-0.5)
    key_vals = projected[..., att_width:2 * att_width]
    value_vals = projected[..., 2 * att_width:3 * att_width]
    gate_logits = projected[..., 3 * att_width:]
    pair_norm = layer_norm(pair_rep)
    pair_bias = jnp.einsum('ijc,ch->hij', pair_norm, pair_bias_w, precision=highest)
    mask_float = row_mask.astype(jnp.float32)
    key_bias = 1000000000.0 * (mask_float - 1.0)

    def attend_row(items):
        query_row, key_row, value_row, bias_row = items
        query_row = query_row.reshape(res_count, head_count, head_depth)
        key_row = key_row.reshape(res_count, head_count, head_depth)
        value_row = value_row.reshape(res_count, head_count, head_depth)
        scores = jnp.einsum('ihd,jhd->hij', query_row, key_row, precision=highest) + pair_bias + bias_row[None, None, :]
        scores = scores - lax.optimization_barrier(jnp.max(scores, axis=-1, keepdims=True))
        weights = jnp.exp(scores)
        weights = weights / lax.optimization_barrier(jnp.sum(weights, axis=-1, keepdims=True))
        mixed = jnp.einsum('hij,jhd->ihd', weights, value_row, precision=highest)
        return mixed.reshape(res_count, att_width)
    attended = lax.map(attend_row, (queries, key_vals, value_vals, key_bias))
    new_alignment = alignment + matmul(attended * jax.nn.sigmoid(gate_logits), attention_out)
    factors = matmul(layer_norm(new_alignment), outer_in) * mask_float[..., None]
    left_outer = factors[..., :outer_width]
    right_outer = factors[..., outer_width:]
    counts = 1.0 + matmul(mask_float.T, mask_float)

    def outer_row(left_row):
        product = jnp.einsum('sp,sjq->jpq', left_row, right_outer, precision=highest)
        return matmul(product.reshape(res_count, outer_width * outer_width), outer_out)
    outer_sum = lax.map(outer_row, jnp.transpose(left_outer, (1, 0, 2)))
    outer_mean = outer_sum / counts[..., None]
    pair_one = pair_rep + outer_mean
    tri_norm = layer_norm(pair_one)
    res_float = residue_mask.astype(jnp.float32)
    pair_valid = (res_float[:, None] * res_float[None, :])[..., None]
    edges = matmul(tri_norm, triangle_in)
    left_edge = jax.nn.sigmoid(edges[..., :inner_width]) * edges[..., inner_width:2 * inner_width] * pair_valid
    right_edge = jax.nn.sigmoid(edges[..., 2 * inner_width:3 * inner_width]) * edges[..., 3 * inner_width:] * pair_valid
    crossed = jnp.einsum('ikc,jkc->ijc', left_edge, right_edge, precision=highest)
    triangle = matmul(layer_norm(crossed), triangle_out) * jax.nn.sigmoid(matmul(tri_norm, triangle_gate))
    pair_mid = pair_one + triangle
    hidden_units = jax.nn.relu(matmul(layer_norm(pair_mid), transit_in))
    new_pair = pair_mid + matmul(hidden_units, transit_out)
    return (new_alignment, new_pair)
```

```python
import functools

import jax
import jax.numpy as jnp
from jax import lax
from jax.experimental import pallas as pl
from jax.experimental.pallas import tpu as pltpu
from jax.sharding import PartitionSpec as P

highest = lax.Precision.HIGHEST
epsilon = 1e-05
f32 = jnp.float32
bf16 = jnp.bfloat16

ROWS = ("branch", "prow")
CHIPS = ("prow", "pcol")
NN = (((1,), (0,)), ((), ()))
NT = (((1,), (1,)), ((), ()))


def layer_norm(values, axis=-1):
    center = values - jnp.mean(values, axis=axis, keepdims=True)
    spread = jnp.mean(center * center, axis=axis, keepdims=True)
    return center * lax.rsqrt(spread + epsilon)


def split(value):
    high = value.astype(bf16)
    low = (value - high.astype(f32)).astype(bf16)
    return high, low


def dot3(left, right, dims=NN):
    left_high, left_low = split(left)
    right_high, right_low = split(right)
    one = functools.partial(lax.dot_general, dimension_numbers=dims, preferred_element_type=f32)
    return one(left_high, right_high) + (one(left_high, right_low) + one(left_low, right_high))


def dot6(left, right, dims=NN):
    return lax.dot_general(left, right, dims, precision=highest, preferred_element_type=f32)


def iota(shape, axis):
    return lax.broadcasted_iota(jnp.int32, shape, axis)


def call(kernel, out_shapes, scratch=(), scalars=0, name=None):
    vmem = pl.BlockSpec(memory_space=pltpu.VMEM)
    smem = pl.BlockSpec(memory_space=pltpu.SMEM)

    def run(*args):
        return pl.pallas_call(
            kernel,
            out_shape=[jax.ShapeDtypeStruct(shape, f32) for shape in out_shapes],
            in_specs=[smem] * scalars + [vmem] * (len(args) - scalars),
            out_specs=[vmem] * len(out_shapes),
            scratch_shapes=list(scratch),
            name=name,
        )(*args)

    return run


def send_kernel(place, pair, align, mask, bias_w, x_send, bias_send):
    pair_norm = layer_norm(pair[...])
    bias = dot6(bias_w[...].T, pair_norm, NT)
    for peer in range(bias_send.shape[0]):
        bias_send[peer] = bias
    normed = layer_norm(align[...])
    lane = iota((8, 256), 1)
    spread = ((lane % 8 == iota((8, 256), 0)) & (lane // 8 == place[0])).astype(f32)
    mask_tile = lax.dot_general(mask[...], spread, NN, preferred_element_type=f32)
    for peer in range(x_send.shape[0]):
        x_send[peer, 0:32] = normed
        x_send[peer, 32:40] = mask_tile


def query_kernel(align, proj, query_out, gate_out):
    normed = layer_norm(align[...])
    query = dot6(normed, proj[:, 0:256]) * 32 ** (-0.5)
    gate_out[...] = jax.nn.sigmoid(dot3(normed, proj[:, 768:1024]))
    own_head = iota((32, 8, 256), 1) == iota((32, 8, 256), 2) // 32
    wide = jnp.where(own_head, jnp.broadcast_to(query[:, None, :], (32, 8, 256)), 0.0)
    query_out[...] = dot6(wide.reshape(256, 256), proj[:, 256:512], NT)


def attend_kernel(
    x_all, bias_all, query, gate, align, mask, mask_col, value_w, out_w, outer_w, new_align, right_send, left_mask, bias_s, mix_s
):
    lane = iota((8, 128), 1)
    chunk = lane // 32
    for i in range(8):
        half, place = divmod(i, 4)
        for group in range(2):
            tile = jnp.zeros((8, 128), f32)
            for c in range(4):
                source = bias_all[group * 4 + c, :, half * 128 : half * 128 + 128]
                shift = ((c - place) * 32) % 128
                if shift:
                    source = pltpu.roll(source, shift, 1)
                tile = jnp.where(chunk == c, source, tile)
            bias_s[i * 8 : i * 8 + 8, group * 128 : group * 128 + 128] = tile
    keys = x_all[0, 32:40, :]
    for r in range(1, 32):
        keys = keys + x_all[r, 32:40, :]
    key_bias = 1000000000.0 * (keys - 1.0)
    for s in range(4):
        x_row = x_all[:, s * 8 : s * 8 + 8, :].reshape(256, 256)
        scores = dot6(query[s * 64 : s * 64 + 64, :], x_row, NT)
        scores = (scores + bias_s[...]) + key_bias[s : s + 1, :]
        weights = jnp.exp(scores - jnp.max(scores, axis=-1, keepdims=True))
        total = jnp.sum(weights, axis=-1, keepdims=True)
        mix_s[s * 64 : s * 64 + 64, :] = dot3(weights, x_row) / total
    values = dot3(mix_s[...], value_w[...]).reshape(32, 8, 256)
    own_head = iota((32, 8, 256), 1) == iota((32, 8, 256), 2) // 32
    mixed = jnp.sum(jnp.where(own_head, values, 0.0), axis=1)
    updated = align[...] + dot3(mixed * gate[...], out_w[...])
    new_align[...] = updated
    factors = dot3(layer_norm(updated), outer_w[...]) * mask_col[...]
    wide_lane = iota((64, 256), 1)
    expand = (iota((64, 256), 0) == wide_lane % 32 + 32 * (wide_lane // 128)).astype(f32)
    wide = dot6(factors, expand)
    left = jnp.zeros((8, 128), f32)
    right = jnp.zeros((8, 128), f32)
    for s in range(4):
        left = jnp.where(chunk == s, wide[s * 8 : s * 8 + 8, 0:128], left)
        right = jnp.where(chunk == s, wide[s * 8 : s * 8 + 8, 128:256], right)
    for peer in range(32):
        right_send[peer] = right
    own = lax.dot_general(mask[...], (lane == iota((8, 128), 0) + 32).astype(f32), NN, preferred_element_type=f32)
    for c in range(8):
        tile = keys[:, (c // 4) * 128 : (c // 4) * 128 + 128]
        shift = (-(c % 4) * 32) % 128
        if shift:
            tile = pltpu.roll(tile, shift, 1)
        left_mask[c, 0:8] = left
        left_mask[c, 8:16] = jnp.where(chunk == 0, tile, own)


def outer_kernel(factors, pair, valid, outer_w, tri_w, pair_one, edge_send, right_s, left_s, sum_s):
    lane = iota((8, 128), 1)
    expand_lane = iota((128, 512), 1)
    expand = (iota((128, 512), 0) == (expand_lane // 128) * 32 + expand_lane % 32).astype(bf16)
    masks = []
    for c in range(8):
        high, low = split(factors[c, 0:32, :])
        wide = lax.dot_general(high, expand, NN, preferred_element_type=f32) + lax.dot_general(low, expand, NN, preferred_element_type=f32)
        left = factors[c, 32:40, :]
        masks.append(factors[c, 40:48, :])
        for s in range(4):
            right_s[c * 4 + s] = wide[:, s * 128 : s * 128 + 128]
            for group in range(8):
                index = s * 32 + group * 4 + lane // 32
                left_s[c * 4 + s, :, group * 128 : group * 128 + 128] = jnp.take_along_axis(left, index, axis=1)

    def one_row(i, carry):
        total = [jnp.zeros((32, 128), f32) for _ in range(8)]
        for s in range(32):
            right = right_s[s]
            row = left_s[s, pl.ds(i, 1), :]
            for group in range(8):
                total[group] = total[group] + right * row[:, group * 128 : group * 128 + 128]
        for group in range(8):
            sum_s[pl.ds(i * 32, 32), group * 128 : group * 128 + 128] = total[group]
        return carry

    lax.fori_loop(0, 8, one_row, 0)
    outer = dot3(sum_s[...], outer_w[...])
    mask_all = jnp.concatenate(masks, axis=0).astype(bf16)
    counts = lax.dot_general(mask_all.T, mask_all, NN, preferred_element_type=f32)
    count = jnp.concatenate([counts[0:32, 32 + i : 33 + i] for i in range(8)], axis=0)
    one = pair[...] + outer / (1.0 + count)
    pair_one[...] = one
    edges = dot3(tri_w[...].T, layer_norm(one), NT)
    left_edge = jax.nn.sigmoid(edges[0:128]) * edges[128:256] * valid[...]
    right_edge = jax.nn.sigmoid(edges[256:384]) * edges[384:512] * valid[...]
    edge_send[:, 0, :] = left_edge[:, 0:128]
    edge_send[:, 1, :] = left_edge[:, 128:256]
    edge_send[:, 2, :] = right_edge[:, 0:128]
    edge_send[:, 3, :] = right_edge[:, 128:256]


def cross_kernel(place, own, other, cross_send, left_s, right_s):
    chunk = iota((16, 128), 1) // 32
    for c in range(8):
        for h in range(2):
            left = own[pl.ds(c * 4 + h, 16, stride=32), :]
            for m in range(4):
                start = (m * 2 + h) * 16
                left_s[start : start + 16, c * 128 : c * 128 + 128] = jnp.where(chunk == m, left, 0.0)
            for half, source in enumerate((own, other)):
                right = source[pl.ds(c * 4 + 2 + h, 16, stride=32), :]
                for m in range(4):
                    part = jnp.where(chunk == m, right, 0.0)
                    part = part + pltpu.roll(part, 32, 1)
                    part = part + pltpu.roll(part, 64, 1)
                    right_s[half, c, pl.ds(h * 4 + m, 16, stride=8), :] = part
    for half in range(2):
        crossed = dot3(left_s[...], jnp.concatenate([right_s[half, c] for c in range(8)], axis=1), NT)
        branch = place[0] if half == 0 else 1 - place[0]
        for c in range(4):
            for h in range(2):
                tile = jnp.zeros((16, 128), f32)
                for m in range(4):
                    part = crossed[(m * 2 + h) * 16 : (m * 2 + h) * 16 + 16, :]
                    shift = ((m - c) * 32) % 128
                    if shift:
                        part = pltpu.roll(part, shift, 1)
                    tile = jnp.where(chunk == m, part, tile)
                cross_send[pl.ds((branch * 4 + c) * 2 + h, 16, stride=16), :] = tile


def gate_kernel(pair_one, gate_w, gate_out):
    gate_out[...] = jax.nn.sigmoid(dot3(layer_norm(pair_one[...]), gate_w[...]))


def final_kernel(crossed, pair_one, gate, out_w, in_w, last_w, new_pair, triangle_s):
    for h in range(2):
        part = layer_norm(crossed[pl.ds(h, 128, stride=2), :], axis=0)
        triangle_s[h * 128 : h * 128 + 128, :] = dot3(part.T, out_w[...])
    middle = pair_one[...] + triangle_s[...] * gate[...]
    hidden = jnp.maximum(dot3(layer_norm(middle), in_w[...]), 0.0)
    new_pair[...] = middle + dot3(hidden, last_w[...])


def shards(
    pair_rep,
    alignment,
    residue_mask,
    row_mask,
    attention_in,
    pair_bias_w,
    attention_out,
    outer_in,
    outer_out,
    triangle_in,
    triangle_gate,
    triangle_out,
    transit_in,
    transit_out,
):
    branch = lax.axis_index("branch").astype(jnp.int32).reshape(1)
    row = lax.axis_index(ROWS).astype(jnp.int32)
    col = lax.axis_index("pcol").astype(jnp.int32)
    pair = pair_rep.reshape(256, 128)
    align = alignment.reshape(32, 256)
    mask_float = row_mask.astype(f32)
    mask = jnp.pad(mask_float, ((0, 4), (0, 0)))
    x_send, bias_send = call(send_kernel, [(16, 40, 256), (8, 8, 256)], scalars=1, name="send")(
        row.reshape(1), pair, align, mask, pair_bias_w
    )
    x_half = lax.all_to_all(x_send, "prow", 0, 0, tiled=True)
    bias_all = lax.all_to_all(bias_send, "pcol", 0, 0, tiled=True)
    query, gate = call(query_kernel, [(256, 256), (32, 256)], name="query")(align, attention_in)
    x_all = lax.all_gather(x_half, "branch", axis=0, tiled=True)
    new_align, right_send, left_mask = call(
        attend_kernel,
        [(32, 256), (32, 8, 128), (8, 16, 128)],
        scratch=[pltpu.VMEM((64, 256), f32), pltpu.VMEM((256, 256), f32)],
        name="attend",
    )(
        x_all,
        bias_all,
        query,
        gate,
        align,
        mask,
        mask_float.reshape(32, 1),
        attention_in[:, 512:768],
        attention_out,
        outer_in,
    )
    right_all = lax.all_to_all(right_send, ROWS, 0, 0, tiled=True)
    factor_send = jnp.concatenate([right_all.reshape(8, 32, 128), left_mask], axis=1)
    factors = lax.all_to_all(factor_send, "pcol", 0, 0, tiled=True)
    res_float = residue_mask.astype(f32)
    row_valid = lax.dynamic_slice_in_dim(res_float, row * 8, 8)
    col_valid = lax.dynamic_slice_in_dim(res_float, col * 32, 32)
    valid = (row_valid[:, None] * col_valid[None, :]).reshape(1, 256)
    pair_one, edge_send = call(
        outer_kernel,
        [(256, 128), (128, 4, 128)],
        scratch=[pltpu.VMEM((32, 32, 128), f32), pltpu.VMEM((32, 8, 1024), f32), pltpu.VMEM((256, 1024), f32)],
        name="outer",
    )(factors, pair, valid, outer_out, triangle_in)
    own_edges = lax.all_to_all(edge_send, CHIPS, 0, 0, tiled=True)
    (tri_gate,) = call(gate_kernel, [(256, 128)], name="gate")(pair_one, triangle_gate)
    other_edges = lax.ppermute(own_edges, "branch", [(0, 1), (1, 0)])
    (cross_send,) = call(
        cross_kernel,
        [(256, 128)],
        scratch=[pltpu.VMEM((128, 1024), f32), pltpu.VMEM((2, 8, 128, 128), f32)],
        scalars=1,
        name="cross",
    )(branch, own_edges.reshape(512, 128), other_edges.reshape(512, 128))
    crossed = lax.all_to_all(cross_send.reshape(128, 2, 128), CHIPS, 0, 0, tiled=True)
    (new_pair,) = call(final_kernel, [(256, 128)], scratch=[pltpu.VMEM((256, 128), f32)], name="final")(
        crossed.reshape(256, 128), pair_one, tri_gate, triangle_out, transit_in, transit_out
    )
    return (new_align.reshape(4, 8, 256), new_pair.reshape(8, 32, 128))


def solution(mesh):
    return jax.shard_map(
        shards,
        mesh=mesh,
        in_specs=(
            P(("branch", "prow"), "pcol", None),
            P("pcol", ("branch", "prow"), None),
            P(),
            P("pcol", ("branch", "prow")),
            P(),
            P(),
            P(),
            P(),
            P(),
            P(),
            P(),
            P(),
            P(),
            P(),
        ),
        out_specs=(P("pcol", ("branch", "prow"), None), P(("branch", "prow"), "pcol", None)),
        check_vma=False,
    )
```

```python
import functools

import jax
import jax.numpy as jnp
from jax import lax
from jax.experimental import pallas as pl
from jax.experimental.pallas import tpu as pltpu
from jax.sharding import PartitionSpec as P


highest = lax.Precision.HIGHEST
epsilon = 1e-05
f32 = jnp.float32
bf16 = jnp.bfloat16

ROWS = ("branch", "prow")
CHIPS = ("prow", "pcol")

NN = (((1,), (0,)), ((), ()))
NT = (((1,), (1,)), ((), ()))


def layer_norm(values, axis=-1):
    center = values - jnp.mean(values, axis=axis, keepdims=True)
    spread = jnp.mean(center * center, axis=axis, keepdims=True)
    return center * lax.rsqrt(spread + epsilon)


def split(value):
    high = value.astype(bf16)
    low = (value - high.astype(f32)).astype(bf16)
    return high, low


def dot3(left, right, dims=NN):
    left_high, left_low = split(left)
    right_high, right_low = split(right)
    one = functools.partial(lax.dot_general, dimension_numbers=dims, preferred_element_type=f32)
    return one(left_high, right_high) + (one(left_high, right_low) + one(left_low, right_high))


def dot6(left, right, dims=NN):
    return lax.dot_general(left, right, dims, precision=highest, preferred_element_type=f32)


def iota(shape, axis):
    return lax.broadcasted_iota(jnp.int32, shape, axis)


def call(kernel, out_shapes, scratch=(), scalars=0, far=0, kept=()):
    vmem = pl.BlockSpec(memory_space=pltpu.VMEM)
    smem = pl.BlockSpec(memory_space=pltpu.SMEM)
    outs = [jax.ShapeDtypeStruct(shape, f32) if n in kept else pltpu.VMEM(shape, f32) for n, shape in enumerate(out_shapes)]

    def run(*args):
        arrays = [pltpu.with_memory_space_constraint(arg, pltpu.VMEM) for arg in args[scalars + far :]]
        return pl.pallas_call(
            kernel,
            out_shape=outs,
            in_specs=[smem] * scalars + [pl.BlockSpec(memory_space=pl.ANY)] * far + [vmem] * len(arrays),
            out_specs=[vmem] * len(out_shapes),
            scratch_shapes=list(scratch),
        )(*args[: scalars + far], *arrays)

    return run


def send_kernel(place, pair, align, mask, bias_w, x_send, bias_send):
    normed = layer_norm(align[...])
    lane = iota((8, 128), 1)
    spread = ((lane % 8 == iota((8, 128), 0)) & (lane // 8 == place[0])).astype(f32)
    mask_rows = jnp.concatenate([mask[...].astype(f32), jnp.zeros((4, 8), f32)], axis=0)
    mask_tile = lax.dot_general(mask_rows, spread, NN, preferred_element_type=f32)
    x_send[0:32] = normed[:, 0:128]
    x_send[32:64] = normed[:, 128:256]
    x_send[64:72] = mask_tile
    bias_send[...] = dot6(bias_w[...], layer_norm(pair[...]), NT)


def query_kernel(place, proj, align, *refs):
    pieces, (query_out, gate_out, bias_out, bias_s, proj_s, gate_s, sems) = refs[:4], refs[4:]
    first = pltpu.make_async_copy(proj.at[:, pl.ds(0, 512)], proj_s, sems.at[0])
    second = pltpu.make_async_copy(proj.at[:, pl.ds(768, 256)], gate_s, sems.at[1])
    first.start()
    second.start()
    for step, piece in enumerate(pieces):
        for high in range(2):
            bias_s[place[1] ^ (step + 4 * high)] = piece[high]
    chunk = iota((8, 128), 1) // 32
    for i in range(8):
        half, spot = divmod(i, 4)
        for group, branch in enumerate((place[0], 1 - place[0])):
            tile = jnp.zeros((8, 128), f32)
            for c in range(4):
                source = bias_s[branch * 4 + c, :, half * 128 : half * 128 + 128]
                shift = ((c - spot) * 32) % 128
                if shift:
                    source = pltpu.roll(source, shift, 1)
                tile = jnp.where(chunk == c, source, tile)
            bias_out[i * 8 : i * 8 + 8, group * 128 : group * 128 + 128] = tile
    normed = layer_norm(align[...])
    first.wait()
    query = dot6(normed, proj_s[:, 0:256]) * 32 ** (-0.5)
    own_head = iota((32, 8, 256), 1) == iota((32, 8, 256), 2) // 32
    wide = jnp.where(own_head, jnp.broadcast_to(query[:, None, :], (32, 8, 256)), 0.0)
    query_out[...] = dot6(wide.reshape(256, 256), proj_s[:, 256:512], NT)
    second.wait()
    gate_out[...] = jax.nn.sigmoid(dot3(normed, gate_s[...]))


def attend_kernel(place, proj, out_w, bias_all, query, gate, align, mask, outer_w, *refs):
    pieces, (new_align, right_send, left_mask, x_s, mix_s, value_s, out_s, sems) = refs[:8], refs[8:]
    value_copy = pltpu.make_async_copy(proj.at[:, pl.ds(512, 256)], value_s, sems.at[0])
    out_copy = pltpu.make_async_copy(out_w, out_s, sems.at[1])
    value_copy.start()
    out_copy.start()
    for index, piece in enumerate(pieces):
        swapped, step = divmod(index, 4)
        for low in range(4):
            x_s[swapped, place[1] ^ (step * 4 + low)] = piece[low]
    x_own, x_other = x_s.at[0], x_s.at[1]
    lane = iota((8, 128), 1)
    chunk = lane // 32
    keys_own, keys_other = x_own[0, 64:72, :], x_other[0, 64:72, :]
    for r in range(1, 16):
        keys_own = keys_own + x_own[r, 64:72, :]
        keys_other = keys_other + x_other[r, 64:72, :]
    key_bias = 1000000000.0 * (jnp.concatenate([keys_own, keys_other], axis=1) - 1.0)
    keys = (jnp.where(place[0] == 0, keys_own, keys_other), jnp.where(place[0] == 0, keys_other, keys_own))
    for s in range(4):
        x_row = jnp.concatenate(
            [
                jnp.concatenate([half[:, t * 32 + s * 8 : t * 32 + s * 8 + 8, :].reshape(128, 128) for t in range(2)], axis=1)
                for half in (x_own, x_other)
            ],
            axis=0,
        )
        scores = dot6(query[s * 64 : s * 64 + 64, :], x_row, NT)
        scores = (scores + bias_all[...]) + key_bias[s : s + 1, :]
        weights = jnp.exp(scores - jnp.max(scores, axis=-1, keepdims=True))
        total = jnp.sum(weights, axis=-1, keepdims=True)
        mix_s[s * 64 : s * 64 + 64, :] = dot3(weights, x_row) / total
    value_copy.wait()
    out_copy.wait()
    values = dot3(mix_s[...], value_s[...]).reshape(32, 8, 256)
    own_head = iota((32, 8, 256), 1) == iota((32, 8, 256), 2) // 32
    mixed = jnp.sum(jnp.where(own_head, values, 0.0), axis=1)
    updated = align[...] + dot3(mixed * gate[...], out_s[...])
    new_align[...] = updated
    mask_rows = jnp.concatenate([mask[...].astype(f32), jnp.zeros((4, 8), f32)], axis=0)
    by_row = (iota((32, 8), 1) == iota((32, 8), 0) // 8).astype(f32)
    mask_wide = lax.dot_general(by_row, mask_rows, NN, preferred_element_type=f32)
    mask_col = jnp.sum(jnp.where(iota((32, 8), 1) == iota((32, 8), 0) % 8, mask_wide, 0.0), axis=1, keepdims=True)
    factors = dot3(layer_norm(updated), outer_w[...], NT) * mask_col
    wide_lane = iota((64, 256), 1)
    expand = (iota((64, 256), 0) == wide_lane % 32 + 32 * (wide_lane // 128)).astype(f32)
    wide = dot6(factors, expand)
    left = jnp.zeros((8, 128), f32)
    right = jnp.zeros((8, 128), f32)
    for s in range(4):
        left = jnp.where(chunk == s, wide[s * 8 : s * 8 + 8, 0:128], left)
        right = jnp.where(chunk == s, wide[s * 8 : s * 8 + 8, 128:256], right)
    for peer in range(32):
        right_send[peer] = right
    own = lax.dot_general(mask_rows, (lane == iota((8, 128), 0) + 32).astype(f32), NN, preferred_element_type=f32)
    for c in range(8):
        tile = keys[c // 4]
        shift = (-(c % 4) * 32) % 128
        if shift:
            tile = pltpu.roll(tile, shift, 1)
        left_mask[c, 0:8] = left
        left_mask[c, 8:16] = jnp.where(chunk == 0, tile, own)


def outer_kernel(factors, pair, valid, outer_w, tri_w, pair_one, edge_send, right_s, left_s, sum_s):
    lane = iota((8, 128), 1)
    expand_lane = iota((128, 512), 1)
    expand = (iota((128, 512), 0) == (expand_lane // 128) * 32 + expand_lane % 32).astype(bf16)
    masks = []
    for c in range(8):
        high, low = split(factors[c, 0:32, :])
        wide = lax.dot_general(high, expand, NN, preferred_element_type=f32) + lax.dot_general(low, expand, NN, preferred_element_type=f32)
        left = factors[c, 32:40, :]
        masks.append(factors[c, 40:48, :])
        for s in range(4):
            right_s[c * 4 + s] = wide[:, s * 128 : s * 128 + 128]
            for group in range(8):
                index = s * 32 + group * 4 + lane // 32
                left_s[c * 4 + s, :, group * 128 : group * 128 + 128] = jnp.take_along_axis(left, index, axis=1)

    def one_row(i, carry):
        total = [jnp.zeros((32, 128), f32) for _ in range(8)]
        for s in range(32):
            right = right_s[s]
            row = left_s[s, pl.ds(i, 1), :]
            for group in range(8):
                total[group] = total[group] + right * row[:, group * 128 : group * 128 + 128]
        for group in range(8):
            sum_s[pl.ds(i * 32, 32), group * 128 : group * 128 + 128] = total[group]
        return carry

    lax.fori_loop(0, 8, one_row, 0)
    outer = dot3(sum_s[...], outer_w[...])
    mask_all = jnp.concatenate(masks, axis=0).astype(bf16)
    counts = lax.dot_general(mask_all.T, mask_all, NN, preferred_element_type=f32)
    count = jnp.concatenate([counts[0:32, 32 + i : 33 + i] for i in range(8)], axis=0)
    one = pair[...] + outer / (1.0 + count)
    pair_one[...] = one
    edges = dot3(tri_w[...].T, layer_norm(one), NT)
    left_edge = jax.nn.sigmoid(edges[0:128]) * edges[128:256] * valid[...]
    right_edge = jax.nn.sigmoid(edges[256:384]) * edges[384:512] * valid[...]
    edge_send[:, 0, :] = left_edge[:, 0:128]
    edge_send[:, 1, :] = left_edge[:, 128:256]
    edge_send[:, 2, :] = right_edge[:, 0:128]
    edge_send[:, 3, :] = right_edge[:, 128:256]


def cross_kernel(place, own, other, cross_send, left_s, right_s):
    chunk = iota((16, 128), 1) // 32
    for c in range(8):
        for h in range(2):
            left = own[pl.ds(c * 4 + h, 16, stride=32), :]
            for m in range(4):
                start = (m * 2 + h) * 16
                left_s[start : start + 16, c * 128 : c * 128 + 128] = jnp.where(chunk == m, left, 0.0)
            for half, source in enumerate((own, other)):
                right = source[pl.ds(c * 4 + 2 + h, 16, stride=32), :]
                for m in range(4):
                    part = jnp.where(chunk == m, right, 0.0)
                    part = part + pltpu.roll(part, 32, 1)
                    part = part + pltpu.roll(part, 64, 1)
                    right_s[half, c, pl.ds(h * 4 + m, 16, stride=8), :] = part
    for half in range(2):
        crossed = dot3(left_s[...], jnp.concatenate([right_s[half, c] for c in range(8)], axis=1), NT)
        branch = place[0] if half == 0 else 1 - place[0]
        for c in range(4):
            for h in range(2):
                tile = jnp.zeros((16, 128), f32)
                for m in range(4):
                    part = crossed[(m * 2 + h) * 16 : (m * 2 + h) * 16 + 16, :]
                    shift = ((m - c) * 32) % 128
                    if shift:
                        part = pltpu.roll(part, shift, 1)
                    tile = jnp.where(chunk == m, part, tile)
                cross_send[pl.ds((branch * 4 + c) * 2 + h, 16, stride=16), :] = tile


def gate_kernel(pair_one, gate_w, gate_out):
    gate_out[...] = jax.nn.sigmoid(dot3(layer_norm(pair_one[...]), gate_w[...]))


def final_kernel(crossed, pair_one, gate, out_w, in_w, last_w, new_pair, triangle_s):
    for h in range(2):
        part = layer_norm(crossed[pl.ds(h, 128, stride=2), :], axis=0)
        triangle_s[h * 128 : h * 128 + 128, :] = dot3(part.T, out_w[...])
    middle = pair_one[...] + triangle_s[...] * gate[...]
    hidden = jnp.maximum(dot3(layer_norm(middle), in_w[...]), 0.0)
    new_pair[...] = middle + dot3(hidden, last_w[...])


def shards(
    pair_rep,
    alignment,
    residue_mask,
    row_mask,
    attention_in,
    pair_bias_w,
    attention_out,
    outer_in,
    outer_out,
    triangle_in,
    triangle_gate,
    triangle_out,
    transit_in,
    transit_out,
):
    branch = lax.axis_index("branch").astype(jnp.int32).reshape(1)
    row = lax.axis_index(ROWS).astype(jnp.int32)
    col = lax.axis_index("pcol").astype(jnp.int32)
    pair = pair_rep.reshape(256, 128)
    align = alignment.reshape(32, 256)
    place = jnp.stack([branch[0], col, row % 16])
    x_send, bias_send = call(send_kernel, [(72, 128), (8, 256)], scalars=1)(
        place[2:3], pair, align, row_mask, pair_bias_w.T
    )

    def swap(value, axis, size, step):
        return lax.ppermute(value, axis, [(d, d ^ step) for d in range(size)])

    x_stack = [x_send] + [swap(x_send, "prow", 16, step) for step in (3, 2, 1)][::-1]
    bias_stack = [bias_send, swap(bias_send, "pcol", 8, 4)]
    x_stack = jnp.stack(x_stack)
    x_own = [x_stack] + [swap(x_stack, "prow", 16, 4 * step) for step in (1, 2, 3)]
    bias_stack = jnp.stack(bias_stack)
    bias_own = [bias_stack] + [swap(bias_stack, "pcol", 8, step) for step in (1, 2, 3)]
    x_other = [swap(value, "branch", 2, 1) for value in x_own]
    query, gate, bias_all = call(
        query_kernel,
        [(256, 256), (32, 256), (64, 256)],
        scratch=[
            pltpu.VMEM((8, 8, 256), f32),
            pltpu.VMEM((256, 512), f32),
            pltpu.VMEM((256, 256), f32),
            pltpu.SemaphoreType.DMA((2,)),
        ],
        scalars=1,
        far=1,
    )(place, attention_in, align, *bias_own)
    new_align, right_send, left_mask = call(
        attend_kernel,
        [(32, 256), (32, 8, 128), (8, 16, 128)],
        scratch=[
            pltpu.VMEM((2, 16, 72, 128), f32),
            pltpu.VMEM((256, 256), f32),
            pltpu.VMEM((256, 256), f32),
            pltpu.VMEM((256, 256), f32),
            pltpu.SemaphoreType.DMA((2,)),
        ],
        scalars=1,
        far=2,
        kept=(0,),
    )(place[::2], attention_in, attention_out, bias_all, query, gate, align, row_mask, outer_in.T, *x_own, *x_other)
    right_all = lax.all_to_all(right_send, ROWS, 0, 0, tiled=True)
    factor_send = jnp.concatenate([right_all.reshape(8, 32, 128), left_mask], axis=1)
    factors = lax.all_to_all(factor_send, "pcol", 0, 0, tiled=True)
    res_float = residue_mask.astype(f32)
    row_valid = lax.dynamic_slice_in_dim(res_float, row * 8, 8)
    col_valid = lax.dynamic_slice_in_dim(res_float, col * 32, 32)
    valid = (row_valid[:, None] * col_valid[None, :]).reshape(1, 256)
    pair_one, edge_send = call(
        outer_kernel,
        [(256, 128), (128, 4, 128)],
        scratch=[pltpu.VMEM((32, 32, 128), f32), pltpu.VMEM((32, 8, 1024), f32), pltpu.VMEM((256, 1024), f32)],
    )(factors, pair, valid, outer_out, triangle_in)
    own_edges = lax.all_to_all(edge_send, CHIPS, 0, 0, tiled=True)
    (tri_gate,) = call(gate_kernel, [(256, 128)])(pair_one, triangle_gate)
    other_edges = lax.ppermute(own_edges, "branch", [(0, 1), (1, 0)])
    (cross_send,) = call(
        cross_kernel, [(256, 128)], scratch=[pltpu.VMEM((128, 1024), f32), pltpu.VMEM((2, 8, 128, 128), f32)], scalars=1
    )(branch, own_edges.reshape(512, 128), other_edges.reshape(512, 128))
    crossed = lax.all_to_all(cross_send.reshape(128, 2, 128), CHIPS, 0, 0, tiled=True)
    (new_pair,) = call(final_kernel, [(256, 128)], scratch=[pltpu.VMEM((256, 128), f32)], kept=(0,))(
        crossed.reshape(256, 128), pair_one, tri_gate, triangle_out, transit_in, transit_out
    )
    return (new_align.reshape(4, 8, 256), new_pair.reshape(8, 32, 128))


def solution(mesh):
    return jax.shard_map(
        shards,
        mesh=mesh,
        in_specs=(
            P(("branch", "prow"), "pcol", None),
            P("pcol", ("branch", "prow"), None),
            P(),
            P("pcol", ("branch", "prow")),
            P(),
            P(),
            P(),
            P(),
            P(),
            P(),
            P(),
            P(),
            P(),
            P(),
        ),
        out_specs=(P("pcol", ("branch", "prow"), None), P(("branch", "prow"), "pcol", None)),
        check_vma=False,
    )
```

```python
import jax
import jax.numpy as jnp
from jax import lax
from jax.experimental import pallas as pl
from jax.experimental.pallas import tpu as pltpu
from jax.sharding import PartitionSpec as P


epsilon = 1e-05
f32 = jnp.float32
bf16 = jnp.bfloat16

ROWS = ("branch", "prow")
CHIPS = ("prow", "pcol")

NN = (((1,), (0,)), ((), ()))
NT = (((1,), (1,)), ((), ()))


def layer_norm(values, axis=-1):
    center = values - jnp.mean(values, axis=axis, keepdims=True)
    spread = jnp.mean(center * center, axis=axis, keepdims=True)
    return center * lax.rsqrt(spread + epsilon)


def split(value):
    high = value.astype(bf16)
    low = (value - high.astype(f32)).astype(bf16)
    return high, low


def stacked_dot(left_parts, right_parts, dims):
    rows = left_parts[0].shape[0]
    terms = []
    for skip, right in enumerate(right_parts):
        used = left_parts[: len(left_parts) - skip]
        wide = used[0] if len(used) == 1 else jnp.concatenate(used, axis=0)
        product = lax.dot_general(wide, right, dims, preferred_element_type=f32)
        terms += [(skip + n, product[n * rows : (n + 1) * rows]) for n in range(len(used))]
    terms.sort(key=lambda term: -term[0])
    total = terms[0][1]
    for _, term in terms[1:]:
        total = total + term
    return total


def split3(value):
    high, rest = value.astype(bf16), value
    rest = rest - high.astype(f32)
    middle = rest.astype(bf16)
    return high, middle, (rest - middle.astype(f32)).astype(bf16)


def dot3(left, right, dims=NN):
    return stacked_dot(split(left), split(right), dims)


def dot6(left, right, dims=NN):
    return stacked_dot(split3(left), split3(right), dims)


def iota(shape, axis):
    return lax.broadcasted_iota(jnp.int32, shape, axis)


def call(kernel, out_shapes, scratch=(), scalars=0, far=0, kept=()):
    vmem = pl.BlockSpec(memory_space=pltpu.VMEM)
    smem = pl.BlockSpec(memory_space=pltpu.SMEM)
    outs = [jax.ShapeDtypeStruct(shape, f32) if n in kept else pltpu.VMEM(shape, f32) for n, shape in enumerate(out_shapes)]

    def run(*args):
        arrays = [pltpu.with_memory_space_constraint(arg, pltpu.VMEM) for arg in args[scalars + far :]]
        return pl.pallas_call(
            kernel,
            out_shape=outs,
            in_specs=[smem] * scalars + [pl.BlockSpec(memory_space=pl.ANY)] * far + [vmem] * len(arrays),
            out_specs=[vmem] * len(out_shapes),
            scratch_shapes=list(scratch),
        )(*args[: scalars + far], *arrays)

    return run


def send_kernel(low, align, mask, x_send):
    normed = layer_norm(align[...])
    lane = iota((8, 128), 1)
    spread = ((lane % 8 == iota((8, 128), 0)) & (lane // 8 == low[0])).astype(f32)
    mask_rows = jnp.concatenate([mask[...].astype(f32), jnp.zeros((4, 8), f32)], axis=0)
    x_send[0:32] = normed[:, 0:128]
    x_send[32:64] = normed[:, 128:256]
    x_send[64:72] = lax.dot_general(mask_rows, spread, NN, preferred_element_type=f32)


def bias_kernel(pair, bias_w, bias_send):
    bias_send[...] = dot6(bias_w[...], layer_norm(pair[...]), NT)


def query_kernel(proj, align, query_out, gate_out, proj_s, gate_s, sems):
    first = pltpu.make_async_copy(proj.at[:, pl.ds(0, 512)], proj_s, sems.at[0])
    second = pltpu.make_async_copy(proj.at[:, pl.ds(768, 256)], gate_s, sems.at[1])
    first.start()
    second.start()
    normed = layer_norm(align[...])
    first.wait()
    query = dot6(normed, proj_s[:, 0:256]) * 32 ** (-0.5)
    own_head = iota((32, 8, 256), 1) == iota((32, 8, 256), 2) // 32
    wide = jnp.where(own_head, jnp.broadcast_to(query[:, None, :], (32, 8, 256)), 0.0)
    query_out[...] = dot6(wide.reshape(256, 256), proj_s[:, 256:512], NT)
    second.wait()
    gate_out[...] = jax.nn.sigmoid(dot3(normed, gate_s[...]))


def attend_kernel(branch_of, col_of, low_of, proj, out_w, query, gate, align, mask, outer_w, *refs):
    bias, pieces = refs[:4], refs[4:12]
    new_align, right_send, left_mask, tiles_s, bias_s, x_s, mix_s, value_s, out_s, sems = refs[12:]
    value_copy = pltpu.make_async_copy(proj.at[:, pl.ds(512, 256)], value_s, sems.at[0])
    out_copy = pltpu.make_async_copy(out_w, out_s, sems.at[1])
    value_copy.start()
    out_copy.start()
    for step, piece in enumerate(bias):
        for high in range(2):
            tiles_s[col_of[0] ^ (step + 4 * high)] = piece[high]
    chunk = iota((8, 128), 1) // 32
    for i in range(8):
        half, spot = divmod(i, 4)
        for group, branch in enumerate((branch_of[0], 1 - branch_of[0])):
            tile = jnp.zeros((8, 128), f32)
            for c in range(4):
                source = tiles_s[branch * 4 + c, :, half * 128 : half * 128 + 128]
                shift = ((c - spot) * 32) % 128
                if shift:
                    source = pltpu.roll(source, shift, 1)
                tile = jnp.where(chunk == c, source, tile)
            bias_s[i * 8 : i * 8 + 8, group * 128 : group * 128 + 128] = tile
    for index, piece in enumerate(pieces):
        swapped, step = divmod(index, 4)
        for low in range(4):
            x_s[swapped, low_of[0] ^ (step * 4 + low)] = piece[low]
    x_own, x_other = x_s.at[0], x_s.at[1]
    lane = iota((8, 128), 1)
    chunk = lane // 32
    keys_own, keys_other = x_own[0, 64:72, :], x_other[0, 64:72, :]
    for r in range(1, 16):
        keys_own = keys_own + x_own[r, 64:72, :]
        keys_other = keys_other + x_other[r, 64:72, :]
    key_bias = 1000000000.0 * (jnp.concatenate([keys_own, keys_other], axis=1) - 1.0)
    keys = (jnp.where(branch_of[0] == 0, keys_own, keys_other), jnp.where(branch_of[0] == 0, keys_other, keys_own))
    for s in range(4):
        x_row = jnp.concatenate(
            [
                jnp.concatenate([half[:, t * 32 + s * 8 : t * 32 + s * 8 + 8, :].reshape(128, 128) for t in range(2)], axis=1)
                for half in (x_own, x_other)
            ],
            axis=0,
        )
        scores = dot6(query[s * 64 : s * 64 + 64, :], x_row, NT)
        scores = (scores + bias_s[...]) + key_bias[s : s + 1, :]
        weights = jnp.exp(scores - jnp.max(scores, axis=-1, keepdims=True))
        total = jnp.sum(weights, axis=-1, keepdims=True)
        mix_s[s * 64 : s * 64 + 64, :] = dot3(weights, x_row) / total
    value_copy.wait()
    out_copy.wait()
    values = dot3(mix_s[...], value_s[...]).reshape(32, 8, 256)
    own_head = iota((32, 8, 256), 1) == iota((32, 8, 256), 2) // 32
    mixed = jnp.sum(jnp.where(own_head, values, 0.0), axis=1)
    updated = align[...] + dot3(mixed * gate[...], out_s[...])
    new_align[...] = updated
    mask_rows = jnp.concatenate([mask[...].astype(f32), jnp.zeros((4, 8), f32)], axis=0)
    by_row = (iota((32, 8), 1) == iota((32, 8), 0) // 8).astype(f32)
    mask_wide = lax.dot_general(by_row, mask_rows, NN, preferred_element_type=f32)
    mask_col = jnp.sum(jnp.where(iota((32, 8), 1) == iota((32, 8), 0) % 8, mask_wide, 0.0), axis=1, keepdims=True)
    factors = dot3(layer_norm(updated), outer_w[...], NT) * mask_col
    wide_lane = iota((64, 256), 1)
    expand = (iota((64, 256), 0) == wide_lane % 32 + 32 * (wide_lane // 128)).astype(f32)
    wide = dot6(factors, expand)
    left = jnp.zeros((8, 128), f32)
    right = jnp.zeros((8, 128), f32)
    for s in range(4):
        left = jnp.where(chunk == s, wide[s * 8 : s * 8 + 8, 0:128], left)
        right = jnp.where(chunk == s, wide[s * 8 : s * 8 + 8, 128:256], right)
    for peer in range(32):
        right_send[peer] = right
    own = lax.dot_general(mask_rows, (lane == iota((8, 128), 0) + 32).astype(f32), NN, preferred_element_type=f32)
    for c in range(8):
        tile = keys[c // 4]
        shift = (-(c % 4) * 32) % 128
        if shift:
            tile = pltpu.roll(tile, shift, 1)
        left_mask[c, 0:8] = left
        left_mask[c, 8:16] = jnp.where(chunk == 0, tile, own)


def outer_kernel(factors, pair, valid, outer_w, tri_w, pair_one, edge_send, right_s, left_s, sum_s):
    lane = iota((8, 128), 1)
    expand_lane = iota((128, 512), 1)
    expand = (iota((128, 512), 0) == (expand_lane // 128) * 32 + expand_lane % 32).astype(bf16)
    rights = factors[:, 0:32, :].reshape(256, 128)
    both = jnp.concatenate(split(rights), axis=0)
    wide = lax.dot_general(both, expand, NN, preferred_element_type=f32)
    wide = (wide[0:256] + wide[256:512]).reshape(8, 32, 512)
    masks = []
    for c in range(8):
        left = factors[c, 32:40, :]
        masks.append(factors[c, 40:48, :])
        for s in range(4):
            right_s[c * 4 + s] = wide[c, :, s * 128 : s * 128 + 128]
            for group in range(8):
                index = s * 32 + group * 4 + lane // 32
                left_s[c * 4 + s, :, group * 128 : group * 128 + 128] = jnp.take_along_axis(left, index, axis=1)

    def one_row(i, carry):
        total = [jnp.zeros((32, 128), f32) for _ in range(8)]
        for s in range(32):
            right = right_s[s]
            row = left_s[s, pl.ds(i, 1), :]
            for group in range(8):
                total[group] = total[group] + right * row[:, group * 128 : group * 128 + 128]
        for group in range(8):
            sum_s[pl.ds(i * 32, 32), group * 128 : group * 128 + 128] = total[group]
        return carry

    lax.fori_loop(0, 8, one_row, 0)
    outer = dot3(sum_s[...], outer_w[...])
    mask_all = jnp.concatenate(masks, axis=0).astype(bf16)
    counts = lax.dot_general(mask_all.T, mask_all, NN, preferred_element_type=f32)
    count = jnp.concatenate([counts[0:32, 32 + i : 33 + i] for i in range(8)], axis=0)
    one = pair[...] + outer / (1.0 + count)
    pair_one[...] = one
    edges = dot3(tri_w[...].T, layer_norm(one), NT)
    left_edge = jax.nn.sigmoid(edges[0:128]) * edges[128:256] * valid[...]
    right_edge = jax.nn.sigmoid(edges[256:384]) * edges[384:512] * valid[...]
    edge_send[:, 0, :] = left_edge[:, 0:128]
    edge_send[:, 1, :] = left_edge[:, 128:256]
    edge_send[:, 2, :] = right_edge[:, 0:128]
    edge_send[:, 3, :] = right_edge[:, 128:256]


def cross_kernel(place, own, other, cross_send, left_s, right_s):
    chunk = iota((16, 128), 1) // 32
    for c in range(8):
        for h in range(2):
            left = own[pl.ds(c * 4 + h, 16, stride=32), :]
            for m in range(4):
                start = (m * 2 + h) * 16
                left_s[start : start + 16, c * 128 : c * 128 + 128] = jnp.where(chunk == m, left, 0.0)
            for half, source in enumerate((own, other)):
                right = source[pl.ds(c * 4 + 2 + h, 16, stride=32), :]
                for m in range(4):
                    part = jnp.where(chunk == m, right, 0.0)
                    part = part + pltpu.roll(part, 32, 1)
                    part = part + pltpu.roll(part, 64, 1)
                    right_s[half, c, pl.ds(h * 4 + m, 16, stride=8), :] = part
    for half in range(2):
        crossed = dot3(left_s[...], jnp.concatenate([right_s[half, c] for c in range(8)], axis=1), NT)
        branch = place[0] if half == 0 else 1 - place[0]
        for c in range(4):
            for h in range(2):
                tile = jnp.zeros((16, 128), f32)
                for m in range(4):
                    part = crossed[(m * 2 + h) * 16 : (m * 2 + h) * 16 + 16, :]
                    shift = ((m - c) * 32) % 128
                    if shift:
                        part = pltpu.roll(part, shift, 1)
                    tile = jnp.where(chunk == m, part, tile)
                cross_send[pl.ds((branch * 4 + c) * 2 + h, 16, stride=16), :] = tile


def gate_kernel(pair_one, gate_w, gate_out):
    gate_out[...] = jax.nn.sigmoid(dot3(layer_norm(pair_one[...]), gate_w[...]))


def final_kernel(crossed, pair_one, gate, out_w, in_w, last_w, new_pair, triangle_s):
    for h in range(2):
        part = layer_norm(crossed[pl.ds(h, 128, stride=2), :], axis=0)
        triangle_s[h * 128 : h * 128 + 128, :] = dot3(part.T, out_w[...])
    middle = pair_one[...] + triangle_s[...] * gate[...]
    hidden = jnp.maximum(dot3(layer_norm(middle), in_w[...]), 0.0)
    new_pair[...] = middle + dot3(hidden, last_w[...])


def shards(
    pair_rep,
    alignment,
    residue_mask,
    row_mask,
    attention_in,
    pair_bias_w,
    attention_out,
    outer_in,
    outer_out,
    triangle_in,
    triangle_gate,
    triangle_out,
    transit_in,
    transit_out,
):
    branch = lax.axis_index("branch").astype(jnp.int32).reshape(1)
    row = lax.axis_index(ROWS).astype(jnp.int32)
    col = lax.axis_index("pcol").astype(jnp.int32)
    pair = pair_rep.reshape(256, 128)
    align = alignment.reshape(32, 256)
    low = lax.axis_index("prow").astype(jnp.int32).reshape(1)
    place = (branch, col.reshape(1), low)
    (x_send,) = call(send_kernel, [(72, 128)], scalars=1)(low, align, row_mask)
    (bias_send,) = call(bias_kernel, [(8, 256)])(pair, pair_bias_w.T)

    def swap(value, axis, size, step):
        return lax.ppermute(value, axis, [(d, d ^ step) for d in range(size)])

    x_stack = [x_send] + [swap(x_send, "prow", 16, step) for step in (3, 2, 1)][::-1]
    bias_stack = [bias_send, swap(bias_send, "pcol", 8, 4)]
    x_stack = jnp.stack(x_stack)
    x_own = [x_stack] + [swap(x_stack, "prow", 16, 4 * step) for step in (1, 2, 3)]
    bias_stack = jnp.stack(bias_stack)
    bias_own = [bias_stack] + [swap(bias_stack, "pcol", 8, step) for step in (1, 2, 3)]
    x_other = [swap(value, "branch", 2, 1) for value in x_own]
    query, gate = call(
        query_kernel,
        [(256, 256), (32, 256)],
        scratch=[pltpu.VMEM((256, 512), f32), pltpu.VMEM((256, 256), f32), pltpu.SemaphoreType.DMA((2,))],
        far=1,
    )(attention_in, align)
    new_align, right_send, left_mask = call(
        attend_kernel,
        [(32, 256), (32, 8, 128), (8, 16, 128)],
        scratch=[
            pltpu.VMEM((8, 8, 256), f32),
            pltpu.VMEM((64, 256), f32),
            pltpu.VMEM((2, 16, 72, 128), f32),
            pltpu.VMEM((256, 256), f32),
            pltpu.VMEM((256, 256), f32),
            pltpu.VMEM((256, 256), f32),
            pltpu.SemaphoreType.DMA((2,)),
        ],
        scalars=3,
        far=2,
        kept=(0,),
    )(*place, attention_in, attention_out, query, gate, align, row_mask, outer_in.T, *bias_own, *x_own, *x_other)
    right_all = lax.all_to_all(right_send, ROWS, 0, 0, tiled=True)
    factor_send = jnp.concatenate([right_all.reshape(8, 32, 128), left_mask], axis=1)
    factors = lax.all_to_all(factor_send, "pcol", 0, 0, tiled=True)
    res_float = residue_mask.astype(f32)
    row_valid = lax.dynamic_slice_in_dim(res_float, row * 8, 8)
    col_valid = lax.dynamic_slice_in_dim(res_float, col * 32, 32)
    valid = (row_valid[:, None] * col_valid[None, :]).reshape(1, 256)
    pair_one, edge_send = call(
        outer_kernel,
        [(256, 128), (128, 4, 128)],
        scratch=[pltpu.VMEM((32, 32, 128), f32), pltpu.VMEM((32, 8, 1024), f32), pltpu.VMEM((256, 1024), f32)],
    )(factors, pair, valid, outer_out, triangle_in)
    own_edges = lax.all_to_all(edge_send, CHIPS, 0, 0, tiled=True)
    (tri_gate,) = call(gate_kernel, [(256, 128)])(pair_one, triangle_gate)
    other_edges = lax.ppermute(own_edges, "branch", [(0, 1), (1, 0)])
    (cross_send,) = call(
        cross_kernel, [(256, 128)], scratch=[pltpu.VMEM((128, 1024), f32), pltpu.VMEM((2, 8, 128, 128), f32)], scalars=1
    )(branch, own_edges.reshape(512, 128), other_edges.reshape(512, 128))
    crossed = lax.all_to_all(cross_send.reshape(128, 2, 128), CHIPS, 0, 0, tiled=True)
    (new_pair,) = call(final_kernel, [(256, 128)], scratch=[pltpu.VMEM((256, 128), f32)], kept=(0,))(
        crossed.reshape(256, 128), pair_one, tri_gate, triangle_out, transit_in, transit_out
    )
    return (new_align.reshape(4, 8, 256), new_pair.reshape(8, 32, 128))


def solution(mesh):
    return jax.shard_map(
        shards,
        mesh=mesh,
        in_specs=(
            P(("branch", "prow"), "pcol", None),
            P("pcol", ("branch", "prow"), None),
            P(),
            P("pcol", ("branch", "prow")),
            P(),
            P(),
            P(),
            P(),
            P(),
            P(),
            P(),
            P(),
            P(),
            P(),
        ),
        out_specs=(P("pcol", ("branch", "prow"), None), P(("branch", "prow"), "pcol", None)),
        check_vma=False,
    )
```

```python
import jax
import jax.numpy as jnp
from jax import lax
from jax.experimental import pallas as pl
from jax.experimental.pallas import tpu as pltpu
from jax.sharding import PartitionSpec as P


epsilon = 1e-05
f32 = jnp.float32
bf16 = jnp.bfloat16

ROWS = ("branch", "prow")
CHIPS = ("prow", "pcol")

NN = (((1,), (0,)), ((), ()))
NT = (((1,), (1,)), ((), ()))


def layer_norm(values, axis=-1):
    center = values - jnp.mean(values, axis=axis, keepdims=True)
    spread = jnp.mean(center * center, axis=axis, keepdims=True)
    return center * lax.rsqrt(spread + epsilon)


def split(value):
    high = value.astype(bf16)
    low = (value - high.astype(f32)).astype(bf16)
    return high, low


def stacked_dot(left_parts, right_parts, dims):
    rows = left_parts[0].shape[0]
    terms = []
    for skip, right in enumerate(right_parts):
        used = left_parts[: len(left_parts) - skip]
        wide = used[0] if len(used) == 1 else jnp.concatenate(used, axis=0)
        product = lax.dot_general(wide, right, dims, preferred_element_type=f32)
        terms += [(skip + n, product[n * rows : (n + 1) * rows]) for n in range(len(used))]
    terms.sort(key=lambda term: -term[0])
    total = terms[0][1]
    for _, term in terms[1:]:
        total = total + term
    return total


def split3(value):
    high, rest = value.astype(bf16), value
    rest = rest - high.astype(f32)
    middle = rest.astype(bf16)
    return high, middle, (rest - middle.astype(f32)).astype(bf16)


def dot3(left, right, dims=NN):
    return stacked_dot(split(left), split(right), dims)


def dot6(left, right, dims=NN):
    return stacked_dot(split3(left), split3(right), dims)


def iota(shape, axis):
    return lax.broadcasted_iota(jnp.int32, shape, axis)


def call(kernel, out_shapes, scratch=(), scalars=0, far=0, loose=0, kept=()):
    vmem = pl.BlockSpec(memory_space=pltpu.VMEM)
    smem = pl.BlockSpec(memory_space=pltpu.SMEM)
    outs = [jax.ShapeDtypeStruct(shape, f32) if n in kept else pltpu.VMEM(shape, f32) for n, shape in enumerate(out_shapes)]

    def run(*args):
        arrays = list(args[scalars + far : scalars + far + loose])
        arrays += [pltpu.with_memory_space_constraint(arg, pltpu.VMEM) for arg in args[scalars + far + loose :]]
        return pl.pallas_call(
            kernel,
            out_shape=outs,
            in_specs=[smem] * scalars + [pl.BlockSpec(memory_space=pl.ANY)] * far + [vmem] * len(arrays),
            out_specs=[vmem] * len(out_shapes),
            scratch_shapes=list(scratch),
        )(*args[: scalars + far], *arrays)

    return run


def send_kernel(low, pair, align, mask, x_send, pair_near, align_near, mask_near, sem):
    copy = pltpu.make_async_copy(pair, pair_near, sem)
    copy.start()
    align_near[...] = align[...]
    normed = layer_norm(align[...])
    lane = iota((8, 128), 1)
    spread = ((lane % 8 == iota((8, 128), 0)) & (lane // 8 == low[0])).astype(f32)
    mask_rows = jnp.concatenate([mask[...].astype(f32), jnp.zeros((4, 8), f32)], axis=0)
    mask_near[...] = mask_rows
    x_send[0:32] = normed[:, 0:128]
    x_send[32:64] = normed[:, 128:256]
    x_send[64:72] = lax.dot_general(mask_rows, spread, NN, preferred_element_type=f32)
    copy.wait()


def bias_kernel(pair, bias_w, bias_send):
    bias_send[...] = dot6(bias_w[...], layer_norm(pair[...]), NT)


def query_kernel(proj, align, query_out, gate_out, proj_s, gate_s, sems):
    first = pltpu.make_async_copy(proj.at[:, pl.ds(0, 512)], proj_s, sems.at[0])
    second = pltpu.make_async_copy(proj.at[:, pl.ds(768, 256)], gate_s, sems.at[1])
    first.start()
    second.start()
    normed = layer_norm(align[...])
    first.wait()
    query = dot6(normed, proj_s[:, 0:256]) * 32 ** (-0.5)
    own_head = iota((32, 8, 256), 1) == iota((32, 8, 256), 2) // 32
    wide = jnp.where(own_head, jnp.broadcast_to(query[:, None, :], (32, 8, 256)), 0.0)
    query_out[...] = dot6(wide.reshape(256, 256), proj_s[:, 256:512], NT)
    second.wait()
    gate_out[...] = jax.nn.sigmoid(dot3(normed, gate_s[...]))


def attend_kernel(branch_of, col_of, low_of, proj, out_w, outer_w, query, gate, align, mask, *refs):
    bias, pieces = refs[:4], refs[4:12]
    new_align, right_send, left_mask, tiles_s, bias_s, x_s, mix_s, value_s, out_s, outer_s, sems = refs[12:]
    outer_copy = pltpu.make_async_copy(outer_w, outer_s, sems.at[2])
    outer_copy.start()
    value_copy = pltpu.make_async_copy(proj.at[:, pl.ds(512, 256)], value_s, sems.at[0])
    out_copy = pltpu.make_async_copy(out_w, out_s, sems.at[1])
    value_copy.start()
    out_copy.start()
    for step, piece in enumerate(bias):
        for high in range(2):
            tiles_s[col_of[0] ^ (step + 4 * high)] = piece[high]
    chunk = iota((8, 128), 1) // 32
    for i in range(8):
        half, spot = divmod(i, 4)
        for group, branch in enumerate((branch_of[0], 1 - branch_of[0])):
            tile = jnp.zeros((8, 128), f32)
            for c in range(4):
                source = tiles_s[branch * 4 + c, :, half * 128 : half * 128 + 128]
                shift = ((c - spot) * 32) % 128
                if shift:
                    source = pltpu.roll(source, shift, 1)
                tile = jnp.where(chunk == c, source, tile)
            bias_s[i * 8 : i * 8 + 8, group * 128 : group * 128 + 128] = tile
    for index, piece in enumerate(pieces):
        swapped, step = divmod(index, 4)
        for low in range(4):
            x_s[swapped, low_of[0] ^ (step * 4 + low)] = piece[low]
    x_own, x_other = x_s.at[0], x_s.at[1]
    lane = iota((8, 128), 1)
    chunk = lane // 32
    keys_own, keys_other = x_own[0, 64:72, :], x_other[0, 64:72, :]
    for r in range(1, 16):
        keys_own = keys_own + x_own[r, 64:72, :]
        keys_other = keys_other + x_other[r, 64:72, :]
    key_bias = 1000000000.0 * (jnp.concatenate([keys_own, keys_other], axis=1) - 1.0)
    keys = (jnp.where(branch_of[0] == 0, keys_own, keys_other), jnp.where(branch_of[0] == 0, keys_other, keys_own))
    x_rows = [
        jnp.concatenate(
            [
                jnp.concatenate([half[:, t * 32 + s * 8 : t * 32 + s * 8 + 8, :].reshape(128, 128) for t in range(2)], axis=1)
                for half in (x_own, x_other)
            ],
            axis=0,
        )
        for s in range(4)
    ]
    x_parts = [split3(x_row) for x_row in x_rows]
    scores = [stacked_dot(split3(query[s * 64 : s * 64 + 64, :]), x_parts[s], NT) for s in range(4)]
    scores = [(scores[s] + bias_s[...]) + key_bias[s : s + 1, :] for s in range(4)]
    weights = [jnp.exp(score - jnp.max(score, axis=-1, keepdims=True)) for score in scores]
    totals = [jnp.sum(weight, axis=-1, keepdims=True) for weight in weights]
    for s in range(4):
        mix_s[s * 64 : s * 64 + 64, :] = stacked_dot(split(weights[s]), x_parts[s][:2], NN) / totals[s]
    value_copy.wait()
    out_copy.wait()
    outer_copy.wait()
    values = dot3(mix_s[...], value_s[...]).reshape(32, 8, 256)
    own_head = iota((32, 8, 256), 1) == iota((32, 8, 256), 2) // 32
    mixed = jnp.sum(jnp.where(own_head, values, 0.0), axis=1)
    updated = align[...] + dot3(mixed * gate[...], out_s[...])
    new_align[...] = updated
    mask_rows = mask[...]
    by_row = (iota((32, 8), 1) == iota((32, 8), 0) // 8).astype(f32)
    mask_wide = lax.dot_general(by_row, mask_rows, NN, preferred_element_type=f32)
    mask_col = jnp.sum(jnp.where(iota((32, 8), 1) == iota((32, 8), 0) % 8, mask_wide, 0.0), axis=1, keepdims=True)
    factors = dot3(layer_norm(updated), outer_s[...], NT) * mask_col
    wide_lane = iota((64, 256), 1)
    right_place = 32 + (wide_lane % 128) // 32 * 8 + wide_lane % 8
    expand = (iota((64, 256), 0) == jnp.where(wide_lane < 128, wide_lane % 32, right_place)).astype(f32)
    wide = dot6(factors, expand)
    left = jnp.zeros((8, 128), f32)
    right = jnp.zeros((8, 128), f32)
    for s in range(4):
        left = jnp.where(chunk == s, wide[s * 8 : s * 8 + 8, 0:128], left)
        right = jnp.where(lane % 32 // 8 == s, wide[s * 8 : s * 8 + 8, 128:256], right)
    for peer in range(32):
        right_send[peer] = right
    own = lax.dot_general(mask_rows, (lane == iota((8, 128), 0) + 32).astype(f32), NN, preferred_element_type=f32)
    for c in range(8):
        tile = keys[c // 4]
        shift = (-(c % 4) * 32) % 128
        if shift:
            tile = pltpu.roll(tile, shift, 1)
        left_mask[c, 0:8] = left
        left_mask[c, 8:16] = jnp.where(chunk == 0, tile, own)


def merge_kernel(right_all, left_mask, merged):
    for c in range(8):
        merged[c, 0:32] = right_all[c * 32 : c * 32 + 32]
        merged[c, 32:48] = left_mask[c]


def outer_kernel(factors, pair, valid, outer_w, tri_w, pair_one, edge_send, right_s, left_s, sum_s):
    lane = iota((8, 128), 1)
    chunk = iota((32, 128), 1) // 32
    for group in range(4):
        for half in range(2):
            tile = jnp.zeros((32, 128), f32)
            for c in range(4):
                source = factors[half * 4 + c, 0:32, :]
                shift = ((c - group) * 32) % 128
                if shift:
                    source = pltpu.roll(source, shift, 1)
                tile = jnp.where(chunk == c, source, tile)
            right_s[group * 32 : group * 32 + 32, half * 128 : half * 128 + 128] = tile
    masks = []
    for c in range(8):
        left = factors[c, 32:40, :]
        masks.append(factors[c, 40:48, :])
        for s in range(4):
            for half in range(2):
                index = s * 32 + half * 16 + lane // 8
                left_s[c * 4 + s, :, half * 128 : half * 128 + 128] = jnp.take_along_axis(left, index, axis=1)
    right_high, right_low = split(right_s[...])
    right_both = jnp.concatenate([right_high, right_low], axis=0)
    diagonal = iota((32, 8, 256), 1) == iota((32, 8, 256), 2) % 8
    for i in range(8):
        rows = jnp.broadcast_to(left_s[:, i : i + 1, :], (32, 8, 256))
        left_high, left_low = split(jnp.where(diagonal, rows, 0.0).reshape(256, 256))
        product = lax.dot_general(right_both, left_high, NN, preferred_element_type=f32)
        product = product[0:128] + (product[128:256] + lax.dot_general(right_high, left_low, NN, preferred_element_type=f32))
        for group in range(4):
            sum_s[i * 32 : i * 32 + 32, group * 256 : group * 256 + 256] = product[group * 32 : group * 32 + 32]
    weights = outer_w[...].reshape(32, 4, 8, 128)
    weights = jnp.concatenate([weights[:, group].reshape(256, 128) for group in range(4)], axis=0)
    outer = dot3(sum_s[...], weights)
    mask_all = jnp.concatenate(masks, axis=0).astype(bf16)
    counts = lax.dot_general(mask_all.T, mask_all, NN, preferred_element_type=f32)
    count = jnp.concatenate([counts[0:32, 32 + i : 33 + i] for i in range(8)], axis=0)
    one = pair[...] + outer / (1.0 + count)
    pair_one[...] = one
    edges = dot3(tri_w[...].T, layer_norm(one), NT)
    left_edge = jax.nn.sigmoid(edges[0:128]) * edges[128:256] * valid[...]
    right_edge = jax.nn.sigmoid(edges[256:384]) * edges[384:512] * valid[...]
    edge_send[:, 0, :] = left_edge[:, 0:128]
    edge_send[:, 1, :] = left_edge[:, 128:256]
    edge_send[:, 2, :] = right_edge[:, 0:128]
    edge_send[:, 3, :] = right_edge[:, 128:256]


def cross_half(left_parts, edges, right_s, store):
    chunk = iota((16, 128), 1) // 32
    for c in range(8):
        for h in range(2):
            right = edges[pl.ds(c * 4 + 2 + h, 16, stride=32), :]
            for m in range(4):
                part = jnp.where(chunk == m, right, 0.0)
                part = part + pltpu.roll(part, 32, 1)
                part = part + pltpu.roll(part, 64, 1)
                right_s[c, pl.ds(h * 4 + m, 16, stride=8), :] = part
    right_parts = split(jnp.concatenate([right_s[c] for c in range(8)], axis=1))
    crossed = stacked_dot(left_parts, right_parts, NT)
    for h in range(2):
        for c in range(4):
            tile = jnp.zeros((16, 128), f32)
            for m in range(4):
                part = crossed[(m * 2 + h) * 16 : (m * 2 + h) * 16 + 16, :]
                shift = ((m - c) * 32) % 128
                if shift:
                    part = pltpu.roll(part, shift, 1)
                tile = jnp.where(chunk == m, part, tile)
            store(c, h, tile)


def cross_kernel(own, left_out, tiles_out, right_s):
    chunk = iota((16, 128), 1) // 32
    for c in range(8):
        for h in range(2):
            left = own[pl.ds(c * 4 + h, 16, stride=32), :]
            for m in range(4):
                start = (m * 2 + h) * 16
                left_out[start : start + 16, c * 128 : c * 128 + 128] = jnp.where(chunk == m, left, 0.0)

    def store(c, h, tile):
        tiles_out[(c * 2 + h) * 16 : (c * 2 + h) * 16 + 16, :] = tile

    cross_half(split(left_out[...]), own, right_s, store)


def cross_rest_kernel(branch_of, left, tiles, other, cross_send, right_s):
    def store_at(branch):
        def store(c, h, tile):
            cross_send[pl.ds((branch * 4 + c) * 2 + h, 16, stride=16), :] = tile

        return store

    store_own = store_at(branch_of[0])
    for c in range(4):
        for h in range(2):
            store_own(c, h, tiles[(c * 2 + h) * 16 : (c * 2 + h) * 16 + 16, :])
    cross_half(split(left[...]), other, right_s, store_at(1 - branch_of[0]))


def gate_kernel(pair_one, gate_w, gate_out):
    gate_out[...] = jax.nn.sigmoid(dot3(layer_norm(pair_one[...]), gate_w[...]))


def final_kernel(crossed, pair_one, gate, out_w, in_w, last_w, new_pair, triangle_s):
    for h in range(2):
        part = layer_norm(crossed[pl.ds(h, 128, stride=2), :], axis=0)
        triangle_s[h * 128 : h * 128 + 128, :] = dot3(part.T, out_w[...])
    middle = pair_one[...] + triangle_s[...] * gate[...]
    hidden = jnp.maximum(dot3(layer_norm(middle), in_w[...]), 0.0)
    new_pair[...] = middle + dot3(hidden, last_w[...])


def shards(
    pair_rep,
    alignment,
    residue_mask,
    row_mask,
    attention_in,
    pair_bias_w,
    attention_out,
    outer_in,
    outer_out,
    triangle_in,
    triangle_gate,
    triangle_out,
    transit_in,
    transit_out,
):
    branch = lax.axis_index("branch").astype(jnp.int32).reshape(1)
    row = lax.axis_index(ROWS).astype(jnp.int32)
    col = lax.axis_index("pcol").astype(jnp.int32)
    pair = pair_rep.reshape(256, 128)
    align = alignment.reshape(32, 256)
    low = lax.axis_index("prow").astype(jnp.int32).reshape(1)
    place = (branch, col.reshape(1), low)
    x_send, pair_near, align_near, mask_near = call(
        send_kernel,
        [(72, 128), (256, 128), (32, 256), (8, 8)],
        scratch=[pltpu.SemaphoreType.DMA],
        scalars=1,
        far=1,
        loose=2,
    )(low, pair, align, row_mask)
    (bias_send,) = call(bias_kernel, [(8, 256)])(pair_near, pair_bias_w.T)

    def swap(value, axis, size, step):
        return lax.ppermute(value, axis, [(d, d ^ step) for d in range(size)])

    x_stack = [x_send] + [swap(x_send, "prow", 16, step) for step in (3, 2, 1)][::-1]
    bias_stack = [bias_send, swap(bias_send, "pcol", 8, 4)]
    x_stack = jnp.stack(x_stack)
    x_own = [x_stack] + [swap(x_stack, "prow", 16, 4 * step) for step in (1, 2, 3)]
    bias_stack = jnp.stack(bias_stack)
    bias_own = [bias_stack] + [swap(bias_stack, "pcol", 8, step) for step in (1, 2, 3)]
    x_other = [swap(value, "branch", 2, 1) for value in x_own]
    query, gate = call(
        query_kernel,
        [(256, 256), (32, 256)],
        scratch=[pltpu.VMEM((256, 512), f32), pltpu.VMEM((256, 256), f32), pltpu.SemaphoreType.DMA((2,))],
        far=1,
    )(attention_in, align_near)
    new_align, right_send, left_mask = call(
        attend_kernel,
        [(32, 256), (32, 8, 128), (8, 16, 128)],
        scratch=[
            pltpu.VMEM((8, 8, 256), f32),
            pltpu.VMEM((64, 256), f32),
            pltpu.VMEM((2, 16, 72, 128), f32),
            pltpu.VMEM((256, 256), f32),
            pltpu.VMEM((256, 256), f32),
            pltpu.VMEM((256, 256), f32),
            pltpu.VMEM((64, 256), f32),
            pltpu.SemaphoreType.DMA((3,)),
        ],
        scalars=3,
        far=3,
        kept=(0,),
    )(*place, attention_in, attention_out, outer_in.T, query, gate, align_near, mask_near, *bias_own, *x_own, *x_other)
    right_all = lax.all_to_all(right_send, ROWS, 0, 0, tiled=True)
    (factor_send,) = call(merge_kernel, [(8, 48, 128)], kept=(0,))(right_all.reshape(256, 128), left_mask)
    factors = lax.all_to_all(factor_send, "pcol", 0, 0, tiled=True)
    res_float = residue_mask.astype(f32)
    row_valid = lax.dynamic_slice_in_dim(res_float, row * 8, 8)
    col_valid = lax.dynamic_slice_in_dim(res_float, col * 32, 32)
    valid = (row_valid[:, None] * col_valid[None, :]).reshape(1, 256)
    pair_one, edge_send = call(
        outer_kernel,
        [(256, 128), (128, 4, 128)],
        scratch=[pltpu.VMEM((128, 256), f32), pltpu.VMEM((32, 8, 256), f32), pltpu.VMEM((256, 1024), f32)],
    )(factors, pair, valid, outer_out, triangle_in)
    own_edges = lax.all_to_all(edge_send, CHIPS, 0, 0, tiled=True)
    (tri_gate,) = call(gate_kernel, [(256, 128)])(pair_one, triangle_gate)
    other_edges = lax.ppermute(own_edges, "branch", [(0, 1), (1, 0)])
    left_wide, tiles = call(
        cross_kernel, [(128, 1024), (128, 128)], scratch=[pltpu.VMEM((8, 128, 128), f32)]
    )(own_edges.reshape(512, 128))
    (cross_send,) = call(
        cross_rest_kernel, [(256, 128)], scratch=[pltpu.VMEM((8, 128, 128), f32)], scalars=1
    )(branch, left_wide, tiles, other_edges.reshape(512, 128))
    crossed = lax.all_to_all(cross_send.reshape(128, 2, 128), CHIPS, 0, 0, tiled=True)
    (new_pair,) = call(final_kernel, [(256, 128)], scratch=[pltpu.VMEM((256, 128), f32)], kept=(0,))(
        crossed.reshape(256, 128), pair_one, tri_gate, triangle_out, transit_in, transit_out
    )
    return (new_align.reshape(4, 8, 256), new_pair.reshape(8, 32, 128))


def solution(mesh):
    return jax.shard_map(
        shards,
        mesh=mesh,
        in_specs=(
            P(("branch", "prow"), "pcol", None),
            P("pcol", ("branch", "prow"), None),
            P(),
            P("pcol", ("branch", "prow")),
            P(),
            P(),
            P(),
            P(),
            P(),
            P(),
            P(),
            P(),
            P(),
            P(),
        ),
        out_specs=(P("pcol", ("branch", "prow"), None), P(("branch", "prow"), "pcol", None)),
        check_vma=False,
    )
```

```python
import jax
import jax.numpy as jnp
from jax import lax
from jax.experimental import pallas as pl
from jax.experimental.pallas import tpu as pltpu
from jax.sharding import PartitionSpec as P


epsilon = 1e-05
f32 = jnp.float32
bf16 = jnp.bfloat16

ROWS = ("branch", "prow")
CHIPS = ("prow", "pcol")

NN = (((1,), (0,)), ((), ()))
NT = (((1,), (1,)), ((), ()))


def layer_norm(values, axis=-1):
    center = values - jnp.mean(values, axis=axis, keepdims=True)
    spread = jnp.mean(center * center, axis=axis, keepdims=True)
    return center * lax.rsqrt(spread + epsilon)


def split(value):
    high = value.astype(bf16)
    low = (value - high.astype(f32)).astype(bf16)
    return high, low


def stacked_dot(left_parts, right_parts, dims):
    rows = left_parts[0].shape[0]
    terms = []
    for skip, right in enumerate(right_parts):
        used = left_parts[: len(left_parts) - skip]
        wide = used[0] if len(used) == 1 else jnp.concatenate(used, axis=0)
        product = lax.dot_general(wide, right, dims, preferred_element_type=f32)
        terms += [(skip + n, product[n * rows : (n + 1) * rows]) for n in range(len(used))]
    terms.sort(key=lambda term: -term[0])
    total = terms[0][1]
    for _, term in terms[1:]:
        total = total + term
    return total


def split3(value):
    high, rest = value.astype(bf16), value
    rest = rest - high.astype(f32)
    middle = rest.astype(bf16)
    return high, middle, (rest - middle.astype(f32)).astype(bf16)


def dot3(left, right, dims=NN):
    return stacked_dot(split(left), split(right), dims)


def dot6(left, right, dims=NN):
    return stacked_dot(split3(left), split3(right), dims)


def iota(shape, axis):
    return lax.broadcasted_iota(jnp.int32, shape, axis)


def call(kernel, out_shapes, scratch=(), scalars=0, far=0, loose=0, kept=()):
    vmem = pl.BlockSpec(memory_space=pltpu.VMEM)
    smem = pl.BlockSpec(memory_space=pltpu.SMEM)
    outs = [jax.ShapeDtypeStruct(shape, f32) if n in kept else pltpu.VMEM(shape, f32) for n, shape in enumerate(out_shapes)]

    def run(*args):
        arrays = list(args[scalars + far : scalars + far + loose])
        arrays += [pltpu.with_memory_space_constraint(arg, pltpu.VMEM) for arg in args[scalars + far + loose :]]
        return pl.pallas_call(
            kernel,
            out_shape=outs,
            in_specs=[smem] * scalars + [pl.BlockSpec(memory_space=pl.ANY)] * far + [vmem] * len(arrays),
            out_specs=[vmem] * len(out_shapes),
            scratch_shapes=list(scratch),
        )(*args[: scalars + far], *arrays)

    return run


def send_kernel(low, pair, align, mask, residues, x_send, pair_near, align_near, mask_near, residues_near, sem):
    copy = pltpu.make_async_copy(pair, pair_near, sem)
    copy.start()
    align_near[...] = align[...]
    normed = layer_norm(align[...])
    lane = iota((8, 128), 1)
    spread = ((lane % 8 == iota((8, 128), 0)) & (lane // 8 == low[0])).astype(f32)
    mask_rows = jnp.concatenate([mask[...].astype(f32), jnp.zeros((4, 8), f32)], axis=0)
    mask_near[...] = mask_rows
    residues_near[...] = residues[...].astype(f32)
    x_send[0:32] = normed[:, 0:128]
    x_send[32:64] = normed[:, 128:256]
    x_send[64:72] = lax.dot_general(mask_rows, spread, NN, preferred_element_type=f32)
    copy.wait()


def bias_kernel(pair, bias_w, bias_send):
    bias_send[...] = dot6(bias_w[...], layer_norm(pair[...]), NT)


def query_kernel(proj, align, query_out, gate_out, proj_s, gate_s, sems):
    first = pltpu.make_async_copy(proj.at[:, pl.ds(0, 512)], proj_s, sems.at[0])
    second = pltpu.make_async_copy(proj.at[:, pl.ds(768, 256)], gate_s, sems.at[1])
    first.start()
    second.start()
    normed = layer_norm(align[...])
    first.wait()
    query = dot6(normed, proj_s[:, 0:256]) * 32 ** (-0.5)
    own_head = iota((32, 8, 256), 1) == iota((32, 8, 256), 2) // 32
    wide = jnp.where(own_head, jnp.broadcast_to(query[:, None, :], (32, 8, 256)), 0.0)
    query_out[...] = dot6(wide.reshape(256, 256), proj_s[:, 256:512], NT)
    second.wait()
    gate_out[...] = jax.nn.sigmoid(dot3(normed, gate_s[...]))


def attend_kernel(branch_of, col_of, low_of, proj, out_w, outer_w, query, gate, align, mask, *refs):
    bias, pieces = refs[:4], refs[4:12]
    new_align, right_send, left_mask, tiles_s, bias_s, x_s, mix_s, value_s, out_s, outer_s, sems = refs[12:]
    outer_copy = pltpu.make_async_copy(outer_w, outer_s, sems.at[2])
    outer_copy.start()
    value_copy = pltpu.make_async_copy(proj.at[:, pl.ds(512, 256)], value_s, sems.at[0])
    out_copy = pltpu.make_async_copy(out_w, out_s, sems.at[1])
    value_copy.start()
    out_copy.start()
    for step, piece in enumerate(bias):
        for high in range(2):
            tiles_s[col_of[0] ^ (step + 4 * high)] = piece[high]
    chunk = iota((8, 128), 1) // 32
    for i in range(8):
        half, spot = divmod(i, 4)
        for group, branch in enumerate((branch_of[0], 1 - branch_of[0])):
            tile = jnp.zeros((8, 128), f32)
            for c in range(4):
                source = tiles_s[branch * 4 + c, :, half * 128 : half * 128 + 128]
                shift = ((c - spot) * 32) % 128
                if shift:
                    source = pltpu.roll(source, shift, 1)
                tile = jnp.where(chunk == c, source, tile)
            bias_s[i * 8 : i * 8 + 8, group * 128 : group * 128 + 128] = tile
    for index, piece in enumerate(pieces):
        swapped, step = divmod(index, 4)
        for low in range(4):
            x_s[swapped, low_of[0] ^ (step * 4 + low)] = piece[low]
    x_own, x_other = x_s.at[0], x_s.at[1]
    lane = iota((8, 128), 1)
    chunk = lane // 32
    keys_own, keys_other = x_own[0, 64:72, :], x_other[0, 64:72, :]
    for r in range(1, 16):
        keys_own = keys_own + x_own[r, 64:72, :]
        keys_other = keys_other + x_other[r, 64:72, :]
    key_bias = 1000000000.0 * (jnp.concatenate([keys_own, keys_other], axis=1) - 1.0)
    keys = (jnp.where(branch_of[0] == 0, keys_own, keys_other), jnp.where(branch_of[0] == 0, keys_other, keys_own))
    x_rows = [
        jnp.concatenate(
            [
                jnp.concatenate([half[:, t * 32 + s * 8 : t * 32 + s * 8 + 8, :].reshape(128, 128) for t in range(2)], axis=1)
                for half in (x_own, x_other)
            ],
            axis=0,
        )
        for s in range(4)
    ]
    x_parts = [split3(x_row) for x_row in x_rows]
    scores = [stacked_dot(split3(query[s * 64 : s * 64 + 64, :]), x_parts[s], NT) for s in range(4)]
    scores = [(scores[s] + bias_s[...]) + key_bias[s : s + 1, :] for s in range(4)]
    weights = [jnp.exp(score - jnp.max(score, axis=-1, keepdims=True)) for score in scores]
    totals = [jnp.sum(weight, axis=-1, keepdims=True) for weight in weights]
    for s in range(4):
        mix_s[s * 64 : s * 64 + 64, :] = stacked_dot(split(weights[s]), x_parts[s][:2], NN) / totals[s]
    value_copy.wait()
    out_copy.wait()
    outer_copy.wait()
    values = dot3(mix_s[...], value_s[...]).reshape(32, 8, 256)
    own_head = iota((32, 8, 256), 1) == iota((32, 8, 256), 2) // 32
    mixed = jnp.sum(jnp.where(own_head, values, 0.0), axis=1)
    updated = align[...] + dot3(mixed * gate[...], out_s[...])
    new_align[...] = updated
    mask_rows = mask[...]
    by_row = (iota((32, 8), 1) == iota((32, 8), 0) // 8).astype(f32)
    mask_wide = lax.dot_general(by_row, mask_rows, NN, preferred_element_type=f32)
    mask_col = jnp.sum(jnp.where(iota((32, 8), 1) == iota((32, 8), 0) % 8, mask_wide, 0.0), axis=1, keepdims=True)
    factors = dot3(layer_norm(updated), outer_s[...], NT) * mask_col
    wide_lane = iota((64, 256), 1)
    right_place = 32 + (wide_lane % 128) // 32 * 8 + wide_lane % 8
    expand = (iota((64, 256), 0) == jnp.where(wide_lane < 128, wide_lane % 32, right_place)).astype(f32)
    wide = dot6(factors, expand)
    left = jnp.zeros((8, 128), f32)
    right = jnp.zeros((8, 128), f32)
    for s in range(4):
        left = jnp.where(chunk == s, wide[s * 8 : s * 8 + 8, 0:128], left)
        right = jnp.where(lane % 32 // 8 == s, wide[s * 8 : s * 8 + 8, 128:256], right)
    for peer in range(32):
        right_send[peer] = right
    own = lax.dot_general(mask_rows, (lane == iota((8, 128), 0) + 32).astype(f32), NN, preferred_element_type=f32)
    for c in range(8):
        tile = keys[c // 4]
        shift = (-(c % 4) * 32) % 128
        if shift:
            tile = pltpu.roll(tile, shift, 1)
        left_mask[c, 0:8] = left
        left_mask[c, 8:16] = jnp.where(chunk == 0, tile, own)


def merge_kernel(right_all, left_mask, merged):
    for c in range(8):
        merged[c, 0:32] = right_all[c * 32 : c * 32 + 32]
        merged[c, 32:48] = left_mask[c]


def outer_kernel(row_of, col_of, factors, pair, residues, outer_w, tri_w, gate_w, pair_one, edge_send, gate_out, right_s, left_s, sum_s):
    lane = iota((8, 128), 1)
    chunk = iota((32, 128), 1) // 32
    for group in range(4):
        for half in range(2):
            tile = jnp.zeros((32, 128), f32)
            for c in range(4):
                source = factors[half * 4 + c, 0:32, :]
                shift = ((c - group) * 32) % 128
                if shift:
                    source = pltpu.roll(source, shift, 1)
                tile = jnp.where(chunk == c, source, tile)
            right_s[group * 32 : group * 32 + 32, half * 128 : half * 128 + 128] = tile
    masks = []
    for c in range(8):
        left = factors[c, 32:40, :]
        masks.append(factors[c, 40:48, :])
        for s in range(4):
            for half in range(2):
                index = s * 32 + half * 16 + lane // 8
                left_s[c * 4 + s, :, half * 128 : half * 128 + 128] = jnp.take_along_axis(left, index, axis=1)
    right_high, right_low = split(right_s[...])
    right_both = jnp.concatenate([right_high, right_low], axis=0)
    diagonal = iota((32, 8, 256), 1) == iota((32, 8, 256), 2) % 8
    for i in range(8):
        rows = jnp.broadcast_to(left_s[:, i : i + 1, :], (32, 8, 256))
        left_high, left_low = split(jnp.where(diagonal, rows, 0.0).reshape(256, 256))
        product = lax.dot_general(right_both, left_high, NN, preferred_element_type=f32)
        product = product[0:128] + (product[128:256] + lax.dot_general(right_high, left_low, NN, preferred_element_type=f32))
        for group in range(4):
            sum_s[i * 32 : i * 32 + 32, group * 256 : group * 256 + 256] = product[group * 32 : group * 32 + 32]
    weights = outer_w[...].reshape(32, 4, 8, 128)
    weights = jnp.concatenate([weights[:, group].reshape(256, 128) for group in range(4)], axis=0)
    outer = dot3(sum_s[...], weights)
    mask_all = jnp.concatenate(masks, axis=0).astype(bf16)
    counts = lax.dot_general(mask_all.T, mask_all, NN, preferred_element_type=f32)
    count = jnp.concatenate([counts[0:32, 32 + i : 33 + i] for i in range(8)], axis=0)
    one = pair[...] + outer / (1.0 + count)
    pair_one[...] = one
    normed = layer_norm(one)
    edges = dot3(tri_w[...].T, normed, NT)
    present = residues[...]
    source, tile = iota((128, 256), 0), iota((128, 256), 1)
    valid = jnp.ones((8, 256), f32)
    for target in (row_of[0] * 8 + tile // 32, col_of[0] * 32 + tile % 32):
        picked = jnp.zeros((8, 256), f32)
        for half in range(2):
            chosen = (source + half * 128 == target).astype(f32)
            wide = jnp.broadcast_to(present[half : half + 1], (8, 128))
            picked = picked + lax.dot_general(wide, chosen, NN, preferred_element_type=f32)
        valid = valid * picked
    valid = valid[0:1]
    left_edge = jax.nn.sigmoid(edges[0:128]) * edges[128:256] * valid
    right_edge = jax.nn.sigmoid(edges[256:384]) * edges[384:512] * valid
    edge_send[:, 0, :] = left_edge[:, 0:128]
    edge_send[:, 1, :] = left_edge[:, 128:256]
    edge_send[:, 2, :] = right_edge[:, 0:128]
    edge_send[:, 3, :] = right_edge[:, 128:256]
    gate_out[...] = jax.nn.sigmoid(dot3(normed, gate_w[...]))


def cross_half(left_parts, edges, right_s, store):
    chunk = iota((16, 128), 1) // 32
    for c in range(8):
        for h in range(2):
            right = edges[pl.ds(c * 4 + 2 + h, 16, stride=32), :]
            for m in range(4):
                part = jnp.where(chunk == m, right, 0.0)
                part = part + pltpu.roll(part, 32, 1)
                part = part + pltpu.roll(part, 64, 1)
                right_s[c, pl.ds(h * 4 + m, 16, stride=8), :] = part
    right_parts = split(jnp.concatenate([right_s[c] for c in range(8)], axis=1))
    crossed = stacked_dot(left_parts, right_parts, NT)
    for h in range(2):
        for c in range(4):
            tile = jnp.zeros((16, 128), f32)
            for m in range(4):
                part = crossed[(m * 2 + h) * 16 : (m * 2 + h) * 16 + 16, :]
                shift = ((m - c) * 32) % 128
                if shift:
                    part = pltpu.roll(part, shift, 1)
                tile = jnp.where(chunk == m, part, tile)
            store(c, h, tile)


def cross_kernel(own, left_out, tiles_out, right_s):
    chunk = iota((16, 128), 1) // 32
    for c in range(8):
        for h in range(2):
            left = own[pl.ds(c * 4 + h, 16, stride=32), :]
            for m in range(4):
                start = (m * 2 + h) * 16
                left_out[start : start + 16, c * 128 : c * 128 + 128] = jnp.where(chunk == m, left, 0.0)

    def store(c, h, tile):
        tiles_out[(c * 2 + h) * 16 : (c * 2 + h) * 16 + 16, :] = tile

    cross_half(split(left_out[...]), own, right_s, store)


def cross_rest_kernel(branch_of, left, tiles, other, cross_send, right_s):
    def store_at(branch):
        def store(c, h, tile):
            cross_send[pl.ds((branch * 4 + c) * 2 + h, 16, stride=16), :] = tile

        return store

    store_own = store_at(branch_of[0])
    for c in range(4):
        for h in range(2):
            store_own(c, h, tiles[(c * 2 + h) * 16 : (c * 2 + h) * 16 + 16, :])
    cross_half(split(left[...]), other, right_s, store_at(1 - branch_of[0]))


def final_kernel(crossed, pair_one, gate, out_w, in_w, last_w, new_pair, triangle_s):
    for h in range(2):
        part = layer_norm(crossed[pl.ds(h, 128, stride=2), :], axis=0)
        triangle_s[h * 128 : h * 128 + 128, :] = dot3(part.T, out_w[...])
    middle = pair_one[...] + triangle_s[...] * gate[...]
    hidden = jnp.maximum(dot3(layer_norm(middle), in_w[...]), 0.0)
    new_pair[...] = middle + dot3(hidden, last_w[...])


def shards(
    pair_rep,
    alignment,
    residue_mask,
    row_mask,
    attention_in,
    pair_bias_w,
    attention_out,
    outer_in,
    outer_out,
    triangle_in,
    triangle_gate,
    triangle_out,
    transit_in,
    transit_out,
):
    branch = lax.axis_index("branch").astype(jnp.int32).reshape(1)
    row = lax.axis_index(ROWS).astype(jnp.int32)
    col = lax.axis_index("pcol").astype(jnp.int32)
    pair = pair_rep.reshape(256, 128)
    align = alignment.reshape(32, 256)
    low = lax.axis_index("prow").astype(jnp.int32).reshape(1)
    place = (branch, col.reshape(1), low)
    x_send, pair_near, align_near, mask_near, residues_near = call(
        send_kernel,
        [(72, 128), (256, 128), (32, 256), (8, 8), (2, 128)],
        scratch=[pltpu.SemaphoreType.DMA],
        scalars=1,
        far=1,
        loose=3,
    )(low, pair, align, row_mask, residue_mask.reshape(2, 128))
    (bias_send,) = call(bias_kernel, [(8, 256)])(pair_near, pair_bias_w.T)

    def swap(value, axis, size, step):
        return lax.ppermute(value, axis, [(d, d ^ step) for d in range(size)])

    x_stack = [x_send] + [swap(x_send, "prow", 16, step) for step in (3, 2, 1)][::-1]
    bias_stack = [bias_send, swap(bias_send, "pcol", 8, 4)]
    x_stack = jnp.stack(x_stack)
    x_own = [x_stack] + [swap(x_stack, "prow", 16, 4 * step) for step in (1, 2, 3)]
    bias_stack = jnp.stack(bias_stack)
    bias_own = [bias_stack] + [swap(bias_stack, "pcol", 8, step) for step in (1, 2, 3)]
    x_other = [swap(value, "branch", 2, 1) for value in x_own]
    query, gate = call(
        query_kernel,
        [(256, 256), (32, 256)],
        scratch=[pltpu.VMEM((256, 512), f32), pltpu.VMEM((256, 256), f32), pltpu.SemaphoreType.DMA((2,))],
        far=1,
    )(attention_in, align_near)
    new_align, right_send, left_mask = call(
        attend_kernel,
        [(32, 256), (32, 8, 128), (8, 16, 128)],
        scratch=[
            pltpu.VMEM((8, 8, 256), f32),
            pltpu.VMEM((64, 256), f32),
            pltpu.VMEM((2, 16, 72, 128), f32),
            pltpu.VMEM((256, 256), f32),
            pltpu.VMEM((256, 256), f32),
            pltpu.VMEM((256, 256), f32),
            pltpu.VMEM((64, 256), f32),
            pltpu.SemaphoreType.DMA((3,)),
        ],
        scalars=3,
        far=3,
        kept=(0,),
    )(*place, attention_in, attention_out, outer_in.T, query, gate, align_near, mask_near, *bias_own, *x_own, *x_other)
    right_all = lax.all_to_all(right_send, ROWS, 0, 0, tiled=True)
    (factor_send,) = call(merge_kernel, [(8, 48, 128)])(right_all.reshape(256, 128), left_mask)
    factors = lax.all_to_all(factor_send, "pcol", 0, 0, tiled=True)
    pair_one, edge_send, tri_gate = call(
        outer_kernel,
        [(256, 128), (128, 4, 128), (256, 128)],
        scratch=[pltpu.VMEM((128, 256), f32), pltpu.VMEM((32, 8, 256), f32), pltpu.VMEM((256, 1024), f32)],
        scalars=2,
    )(row.reshape(1), col.reshape(1), factors, pair, residues_near, outer_out, triangle_in, triangle_gate)
    own_edges = lax.all_to_all(edge_send, CHIPS, 0, 0, tiled=True)
    other_edges = lax.ppermute(own_edges, "branch", [(0, 1), (1, 0)])
    left_wide, tiles = call(
        cross_kernel, [(128, 1024), (128, 128)], scratch=[pltpu.VMEM((8, 128, 128), f32)]
    )(own_edges.reshape(512, 128))
    (cross_send,) = call(
        cross_rest_kernel, [(256, 128)], scratch=[pltpu.VMEM((8, 128, 128), f32)], scalars=1
    )(branch, left_wide, tiles, other_edges.reshape(512, 128))
    crossed = lax.all_to_all(cross_send.reshape(128, 2, 128), CHIPS, 0, 0, tiled=True)
    (new_pair,) = call(final_kernel, [(256, 128)], scratch=[pltpu.VMEM((256, 128), f32)], kept=(0,))(
        crossed.reshape(256, 128), pair_one, tri_gate, triangle_out, transit_in, transit_out
    )
    return (new_align.reshape(4, 8, 256), new_pair.reshape(8, 32, 128))


def solution(mesh):
    return jax.shard_map(
        shards,
        mesh=mesh,
        in_specs=(
            P(("branch", "prow"), "pcol", None),
            P("pcol", ("branch", "prow"), None),
            P(),
            P("pcol", ("branch", "prow")),
            P(),
            P(),
            P(),
            P(),
            P(),
            P(),
            P(),
            P(),
            P(),
            P(),
        ),
        out_specs=(P("pcol", ("branch", "prow"), None), P(("branch", "prow"), "pcol", None)),
        check_vma=False,
    )
```

```python
import jax
import jax.numpy as jnp
from jax import lax
from jax.experimental import pallas as pl
from jax.experimental.pallas import tpu as pltpu
from jax.sharding import PartitionSpec as P


epsilon = 1e-05
f32 = jnp.float32
bf16 = jnp.bfloat16

ROWS = ("branch", "prow")
CHIPS = ("prow", "pcol")

NN = (((1,), (0,)), ((), ()))
NT = (((1,), (1,)), ((), ()))


def layer_norm(values, axis=-1):
    center = values - jnp.mean(values, axis=axis, keepdims=True)
    spread = jnp.mean(center * center, axis=axis, keepdims=True)
    return center * lax.rsqrt(spread + epsilon)


def split(value):
    high = value.astype(bf16)
    low = (value - high.astype(f32)).astype(bf16)
    return high, low


def stacked_dot(left_parts, right_parts, dims):
    rows = left_parts[0].shape[0]
    terms = []
    for skip, right in enumerate(right_parts):
        used = left_parts[: len(left_parts) - skip]
        wide = used[0] if len(used) == 1 else jnp.concatenate(used, axis=0)
        product = lax.dot_general(wide, right, dims, preferred_element_type=f32)
        terms += [(skip + n, product[n * rows : (n + 1) * rows]) for n in range(len(used))]
    terms.sort(key=lambda term: -term[0])
    total = terms[0][1]
    for _, term in terms[1:]:
        total = total + term
    return total


def split3(value):
    high, rest = value.astype(bf16), value
    rest = rest - high.astype(f32)
    middle = rest.astype(bf16)
    return high, middle, (rest - middle.astype(f32)).astype(bf16)


def dot3(left, right, dims=NN):
    return stacked_dot(split(left), split(right), dims)


def dot6(left, right, dims=NN):
    return stacked_dot(split3(left), split3(right), dims)


def iota(shape, axis):
    return lax.broadcasted_iota(jnp.int32, shape, axis)


def call(kernel, out_shapes, scratch=(), scalars=0, far=0, loose=0, kept=()):
    vmem = pl.BlockSpec(memory_space=pltpu.VMEM)
    smem = pl.BlockSpec(memory_space=pltpu.SMEM)
    outs = [jax.ShapeDtypeStruct(shape, f32) if n in kept else pltpu.VMEM(shape, f32) for n, shape in enumerate(out_shapes)]

    def run(*args):
        arrays = list(args[scalars + far : scalars + far + loose])
        arrays += [pltpu.with_memory_space_constraint(arg, pltpu.VMEM) for arg in args[scalars + far + loose :]]
        return pl.pallas_call(
            kernel,
            out_shape=outs,
            in_specs=[smem] * scalars + [pl.BlockSpec(memory_space=pl.ANY)] * far + [vmem] * len(arrays),
            out_specs=[vmem] * len(out_shapes),
            scratch_shapes=list(scratch),
        )(*args[: scalars + far], *arrays)

    return run


def send_kernel(low, pair, align, mask, residues, x_send, pair_near, align_near, mask_near, residues_near, sem):
    copy = pltpu.make_async_copy(pair, pair_near, sem)
    copy.start()
    align_near[...] = align[...]
    normed = layer_norm(align[...])
    lane = iota((8, 128), 1)
    spread = ((lane % 8 == iota((8, 128), 0)) & (lane // 8 == low[0])).astype(f32)
    mask_rows = jnp.concatenate([mask[...].astype(f32), jnp.zeros((4, 8), f32)], axis=0)
    mask_near[...] = mask_rows
    residues_near[...] = residues[...].astype(f32)
    x_send[0:32] = normed[:, 0:128]
    x_send[32:64] = normed[:, 128:256]
    x_send[64:72] = lax.dot_general(mask_rows, spread, NN, preferred_element_type=f32)
    copy.wait()


def bias_kernel(pair, bias_w, bias_send):
    bias_send[...] = dot6(bias_w[...], layer_norm(pair[...]), NT)


def query_kernel(proj, align, query_out, gate_out, proj_s, gate_s, sems):
    first = pltpu.make_async_copy(proj.at[:, pl.ds(0, 512)], proj_s, sems.at[0])
    second = pltpu.make_async_copy(proj.at[:, pl.ds(768, 256)], gate_s, sems.at[1])
    first.start()
    second.start()
    normed = layer_norm(align[...])
    first.wait()
    query = dot6(normed, proj_s[:, 0:256]) * 32 ** (-0.5)
    own_head = iota((32, 8, 256), 1) == iota((32, 8, 256), 2) // 32
    wide = jnp.where(own_head, jnp.broadcast_to(query[:, None, :], (32, 8, 256)), 0.0)
    query_out[...] = dot6(wide.reshape(256, 256), proj_s[:, 256:512], NT)
    second.wait()
    gate_out[...] = jax.nn.sigmoid(dot3(normed, gate_s[...]))


def attend_kernel(branch_of, col_of, low_of, proj, out_w, outer_w, query, gate, align, mask, *refs):
    bias, pieces = refs[:4], refs[4:12]
    new_align, right_send, left_mask, tiles_s, bias_s, x_s, mix_s, value_s, out_s, outer_s, sems = refs[12:]
    outer_copy = pltpu.make_async_copy(outer_w, outer_s, sems.at[2])
    outer_copy.start()
    value_copy = pltpu.make_async_copy(proj.at[:, pl.ds(512, 256)], value_s, sems.at[0])
    out_copy = pltpu.make_async_copy(out_w, out_s, sems.at[1])
    value_copy.start()
    out_copy.start()
    for step, piece in enumerate(bias):
        for high in range(2):
            tiles_s[col_of[0] ^ (step + 4 * high)] = piece[high]
    chunk = iota((8, 128), 1) // 32
    for i in range(8):
        half, spot = divmod(i, 4)
        for group, branch in enumerate((branch_of[0], 1 - branch_of[0])):
            tile = jnp.zeros((8, 128), f32)
            for c in range(4):
                source = tiles_s[branch * 4 + c, :, half * 128 : half * 128 + 128]
                shift = ((c - spot) * 32) % 128
                if shift:
                    source = pltpu.roll(source, shift, 1)
                tile = jnp.where(chunk == c, source, tile)
            bias_s[i * 8 : i * 8 + 8, group * 128 : group * 128 + 128] = tile
    for index, piece in enumerate(pieces):
        swapped, step = divmod(index, 4)
        for low in range(4):
            x_s[swapped, low_of[0] ^ (step * 4 + low)] = piece[low]
    x_own, x_other = x_s.at[0], x_s.at[1]
    lane = iota((8, 128), 1)
    chunk = lane // 32
    keys_own, keys_other = x_own[0, 64:72, :], x_other[0, 64:72, :]
    for r in range(1, 16):
        keys_own = keys_own + x_own[r, 64:72, :]
        keys_other = keys_other + x_other[r, 64:72, :]
    key_bias = 1000000000.0 * (jnp.concatenate([keys_own, keys_other], axis=1) - 1.0)
    keys = (jnp.where(branch_of[0] == 0, keys_own, keys_other), jnp.where(branch_of[0] == 0, keys_other, keys_own))
    x_rows = [
        jnp.concatenate(
            [
                jnp.concatenate([half[:, t * 32 + s * 8 : t * 32 + s * 8 + 8, :].reshape(128, 128) for t in range(2)], axis=1)
                for half in (x_own, x_other)
            ],
            axis=0,
        )
        for s in range(4)
    ]
    x_parts = [split3(x_row) for x_row in x_rows]
    scores = [stacked_dot(split3(query[s * 64 : s * 64 + 64, :]), x_parts[s], NT) for s in range(4)]
    scores = [(scores[s] + bias_s[...]) + key_bias[s : s + 1, :] for s in range(4)]
    weights = [jnp.exp(score - jnp.max(score, axis=-1, keepdims=True)) for score in scores]
    totals = [jnp.sum(weight, axis=-1, keepdims=True) for weight in weights]
    for s in range(4):
        mix_s[s * 64 : s * 64 + 64, :] = stacked_dot(split(weights[s]), x_parts[s][:2], NN) / totals[s]
    value_copy.wait()
    out_copy.wait()
    outer_copy.wait()
    values = dot3(mix_s[...], value_s[...]).reshape(32, 8, 256)
    own_head = iota((32, 8, 256), 1) == iota((32, 8, 256), 2) // 32
    mixed = jnp.sum(jnp.where(own_head, values, 0.0), axis=1)
    updated = align[...] + dot3(mixed * gate[...], out_s[...])
    new_align[...] = updated
    mask_rows = mask[...]
    by_row = (iota((32, 8), 1) == iota((32, 8), 0) // 8).astype(f32)
    mask_wide = lax.dot_general(by_row, mask_rows, NN, preferred_element_type=f32)
    mask_col = jnp.sum(jnp.where(iota((32, 8), 1) == iota((32, 8), 0) % 8, mask_wide, 0.0), axis=1, keepdims=True)
    factors = dot3(layer_norm(updated), outer_s[...], NT) * mask_col
    wide_lane = iota((64, 256), 1)
    right_place = 32 + (wide_lane % 128) // 32 * 8 + wide_lane % 8
    expand = (iota((64, 256), 0) == jnp.where(wide_lane < 128, wide_lane % 32, right_place)).astype(f32)
    wide = dot6(factors, expand)
    left = jnp.zeros((8, 128), f32)
    right = jnp.zeros((8, 128), f32)
    for s in range(4):
        left = jnp.where(chunk == s, wide[s * 8 : s * 8 + 8, 0:128], left)
        right = jnp.where(lane % 32 // 8 == s, wide[s * 8 : s * 8 + 8, 128:256], right)
    for peer in range(32):
        right_send[peer] = right
    own = lax.dot_general(mask_rows, (lane == iota((8, 128), 0) + 32).astype(f32), NN, preferred_element_type=f32)
    for c in range(8):
        tile = keys[c // 4]
        shift = (-(c % 4) * 32) % 128
        if shift:
            tile = pltpu.roll(tile, shift, 1)
        left_mask[c, 0:8] = left
        left_mask[c, 8:16] = jnp.where(chunk == 0, tile, own)


def merge_kernel(right_all, left_mask, merged):
    for c in range(8):
        merged[c, 0:32] = right_all[c * 32 : c * 32 + 32]
        merged[c, 32:48] = left_mask[c]


def outer_kernel(branch_of, low_of, col_of, factors, pair, residues, outer_w, tri_w, gate_w, pair_one, edge_send, gate_out, right_s, left_s, sum_s):
    lane = iota((8, 128), 1)
    chunk = iota((32, 128), 1) // 32
    for group in range(4):
        for half in range(2):
            tile = jnp.zeros((32, 128), f32)
            for c in range(4):
                source = factors[half * 4 + c, 0:32, :]
                shift = ((c - group) * 32) % 128
                if shift:
                    source = pltpu.roll(source, shift, 1)
                tile = jnp.where(chunk == c, source, tile)
            right_s[group * 32 : group * 32 + 32, half * 128 : half * 128 + 128] = tile
    masks = []
    for c in range(8):
        left = factors[c, 32:40, :]
        masks.append(factors[c, 40:48, :])
        for s in range(4):
            for half in range(2):
                index = s * 32 + half * 16 + lane // 8
                left_s[c * 4 + s, :, half * 128 : half * 128 + 128] = jnp.take_along_axis(left, index, axis=1)
    right_high, right_low = split(right_s[...])
    right_both = jnp.concatenate([right_high, right_low], axis=0)
    diagonal = iota((32, 8, 256), 1) == iota((32, 8, 256), 2) % 8
    for i in range(8):
        rows = jnp.broadcast_to(left_s[:, i : i + 1, :], (32, 8, 256))
        left_high, left_low = split(jnp.where(diagonal, rows, 0.0).reshape(256, 256))
        product = lax.dot_general(right_both, left_high, NN, preferred_element_type=f32)
        product = product[0:128] + (product[128:256] + lax.dot_general(right_high, left_low, NN, preferred_element_type=f32))
        for group in range(4):
            sum_s[i * 32 : i * 32 + 32, group * 256 : group * 256 + 256] = product[group * 32 : group * 32 + 32]
    weights = outer_w[...].reshape(32, 4, 8, 128)
    weights = jnp.concatenate([weights[:, group].reshape(256, 128) for group in range(4)], axis=0)
    outer = dot3(sum_s[...], weights)
    mask_all = jnp.concatenate(masks, axis=0).astype(bf16)
    counts = lax.dot_general(mask_all.T, mask_all, NN, preferred_element_type=f32)
    count = jnp.concatenate([counts[0:32, 32 + i : 33 + i] for i in range(8)], axis=0)
    one = pair[...] + outer / (1.0 + count)
    pair_one[...] = one
    normed = layer_norm(one)
    edges = dot3(tri_w[...].T, normed, NT)
    present = residues[...]
    source, tile = iota((128, 256), 0), iota((128, 256), 1)
    valid = jnp.ones((8, 256), f32)
    for target in ((branch_of[0] * 16 + low_of[0]) * 8 + tile // 32, col_of[0] * 32 + tile % 32):
        picked = jnp.zeros((8, 256), f32)
        for half in range(2):
            chosen = (source + half * 128 == target).astype(f32)
            wide = jnp.broadcast_to(present[half : half + 1], (8, 128))
            picked = picked + lax.dot_general(wide, chosen, NN, preferred_element_type=f32)
        valid = valid * picked
    valid = valid[0:1]
    left_edge = jax.nn.sigmoid(edges[0:128]) * edges[128:256] * valid
    right_edge = jax.nn.sigmoid(edges[256:384]) * edges[384:512] * valid
    edge_send[:, 0, :] = left_edge[:, 0:128]
    edge_send[:, 1, :] = left_edge[:, 128:256]
    edge_send[:, 2, :] = right_edge[:, 0:128]
    edge_send[:, 3, :] = right_edge[:, 128:256]
    gate_out[...] = jax.nn.sigmoid(dot3(normed, gate_w[...]))


def cross_half(left_parts, edges, right_s, store):
    chunk = iota((16, 128), 1) // 32
    for c in range(8):
        for h in range(2):
            right = edges[pl.ds(c * 4 + 2 + h, 16, stride=32), :]
            for m in range(4):
                part = jnp.where(chunk == m, right, 0.0)
                part = part + pltpu.roll(part, 32, 1)
                part = part + pltpu.roll(part, 64, 1)
                right_s[c, pl.ds(h * 4 + m, 16, stride=8), :] = part
    right_parts = split(jnp.concatenate([right_s[c] for c in range(8)], axis=1))
    crossed = stacked_dot(left_parts, right_parts, NT)
    for h in range(2):
        for c in range(4):
            tile = jnp.zeros((16, 128), f32)
            for m in range(4):
                part = crossed[(m * 2 + h) * 16 : (m * 2 + h) * 16 + 16, :]
                shift = ((m - c) * 32) % 128
                if shift:
                    part = pltpu.roll(part, shift, 1)
                tile = jnp.where(chunk == m, part, tile)
            store(c, h, tile)


def cross_kernel(own, left_out, tiles_out, right_s):
    chunk = iota((16, 128), 1) // 32
    for c in range(8):
        for h in range(2):
            left = own[pl.ds(c * 4 + h, 16, stride=32), :]
            for m in range(4):
                start = (m * 2 + h) * 16
                left_out[start : start + 16, c * 128 : c * 128 + 128] = jnp.where(chunk == m, left, 0.0)

    def store(c, h, tile):
        tiles_out[(c * 2 + h) * 16 : (c * 2 + h) * 16 + 16, :] = tile

    cross_half(split(left_out[...]), own, right_s, store)


def cross_rest_kernel(branch_of, left, tiles, other, cross_send, right_s):
    def store_at(branch):
        def store(c, h, tile):
            cross_send[pl.ds((branch * 4 + c) * 2 + h, 16, stride=16), :] = tile

        return store

    store_own = store_at(branch_of[0])
    for c in range(4):
        for h in range(2):
            store_own(c, h, tiles[(c * 2 + h) * 16 : (c * 2 + h) * 16 + 16, :])
    cross_half(split(left[...]), other, right_s, store_at(1 - branch_of[0]))


def final_kernel(crossed, pair_one, gate, out_w, in_w, last_w, new_pair, triangle_s):
    for h in range(2):
        part = layer_norm(crossed[pl.ds(h, 128, stride=2), :], axis=0)
        triangle_s[h * 128 : h * 128 + 128, :] = dot3(part.T, out_w[...])
    middle = pair_one[...] + triangle_s[...] * gate[...]
    hidden = jnp.maximum(dot3(layer_norm(middle), in_w[...]), 0.0)
    new_pair[...] = middle + dot3(hidden, last_w[...])


def shards(
    pair_rep,
    alignment,
    residue_mask,
    row_mask,
    attention_in,
    pair_bias_w,
    attention_out,
    outer_in,
    outer_out,
    triangle_in,
    triangle_gate,
    triangle_out,
    transit_in,
    transit_out,
):
    branch = lax.axis_index("branch").astype(jnp.int32).reshape(1)
    col = lax.axis_index("pcol").astype(jnp.int32)
    pair = pair_rep.reshape(256, 128)
    align = alignment.reshape(32, 256)
    low = lax.axis_index("prow").astype(jnp.int32).reshape(1)
    place = (branch, col.reshape(1), low)
    x_send, pair_near, align_near, mask_near, residues_near = call(
        send_kernel,
        [(72, 128), (256, 128), (32, 256), (8, 8), (2, 128)],
        scratch=[pltpu.SemaphoreType.DMA],
        scalars=1,
        far=1,
        loose=3,
    )(low, pair, align, row_mask, residue_mask.reshape(2, 128))
    (bias_send,) = call(bias_kernel, [(8, 256)])(pair_near, pair_bias_w.T)

    def swap(value, axis, size, step):
        return lax.ppermute(value, axis, [(d, d ^ step) for d in range(size)])

    x_stack = [x_send] + [swap(x_send, "prow", 16, step) for step in (3, 2, 1)][::-1]
    bias_stack = [bias_send, swap(bias_send, "pcol", 8, 4)]
    x_stack = jnp.stack(x_stack)
    x_own = [x_stack] + [swap(x_stack, "prow", 16, 4 * step) for step in (1, 2, 3)]
    bias_stack = jnp.stack(bias_stack)
    bias_own = [bias_stack] + [swap(bias_stack, "pcol", 8, step) for step in (1, 2, 3)]
    x_other = [swap(value, "branch", 2, 1) for value in x_own]
    query, gate = call(
        query_kernel,
        [(256, 256), (32, 256)],
        scratch=[pltpu.VMEM((256, 512), f32), pltpu.VMEM((256, 256), f32), pltpu.SemaphoreType.DMA((2,))],
        far=1,
    )(attention_in, align_near)
    new_align, right_send, left_mask = call(
        attend_kernel,
        [(32, 256), (32, 8, 128), (8, 16, 128)],
        scratch=[
            pltpu.VMEM((8, 8, 256), f32),
            pltpu.VMEM((64, 256), f32),
            pltpu.VMEM((2, 16, 72, 128), f32),
            pltpu.VMEM((256, 256), f32),
            pltpu.VMEM((256, 256), f32),
            pltpu.VMEM((256, 256), f32),
            pltpu.VMEM((64, 256), f32),
            pltpu.SemaphoreType.DMA((3,)),
        ],
        scalars=3,
        far=3,
        kept=(0,),
    )(*place, attention_in, attention_out, outer_in.T, query, gate, align_near, mask_near, *bias_own, *x_own, *x_other)
    right_all = lax.all_to_all(right_send, ROWS, 0, 0, tiled=True)
    (factor_send,) = call(merge_kernel, [(8, 48, 128)])(right_all.reshape(256, 128), left_mask)
    factors = lax.all_to_all(factor_send, "pcol", 0, 0, tiled=True)
    pair_one, edge_send, tri_gate = call(
        outer_kernel,
        [(256, 128), (128, 4, 128), (256, 128)],
        scratch=[pltpu.VMEM((128, 256), f32), pltpu.VMEM((32, 8, 256), f32), pltpu.VMEM((256, 1024), f32)],
        scalars=3,
    )(branch, low, col.reshape(1), factors, pair, residues_near, outer_out, triangle_in, triangle_gate)
    own_edges = lax.all_to_all(edge_send, CHIPS, 0, 0, tiled=True)
    other_edges = lax.ppermute(own_edges, "branch", [(0, 1), (1, 0)])
    left_wide, tiles = call(
        cross_kernel, [(128, 1024), (128, 128)], scratch=[pltpu.VMEM((8, 128, 128), f32)]
    )(own_edges.reshape(512, 128))
    (cross_send,) = call(
        cross_rest_kernel, [(256, 128)], scratch=[pltpu.VMEM((8, 128, 128), f32)], scalars=1
    )(branch, left_wide, tiles, other_edges.reshape(512, 128))
    crossed = lax.all_to_all(cross_send.reshape(128, 2, 128), CHIPS, 0, 0, tiled=True)
    (new_pair,) = call(final_kernel, [(256, 128)], scratch=[pltpu.VMEM((256, 128), f32)], kept=(0,))(
        crossed.reshape(256, 128), pair_one, tri_gate, triangle_out, transit_in, transit_out
    )
    return (new_align.reshape(4, 8, 256), new_pair.reshape(8, 32, 128))


def solution(mesh):
    return jax.shard_map(
        shards,
        mesh=mesh,
        in_specs=(
            P(("branch", "prow"), "pcol", None),
            P("pcol", ("branch", "prow"), None),
            P(),
            P("pcol", ("branch", "prow")),
            P(),
            P(),
            P(),
            P(),
            P(),
            P(),
            P(),
            P(),
            P(),
            P(),
        ),
        out_specs=(P("pcol", ("branch", "prow"), None), P(("branch", "prow"), "pcol", None)),
        check_vma=False,
    )
```
